32 devices in a mesh: sub: 16 (over z, x, core), grid: 2 (over y).
Axes of the slice: x: 2, y: 2, z: 4, core: 2. Of those that a mesh axis runs over, the one named last changes fastest.
Arguments:
- front_entries: float32 [16, 12, 128, 2, 1536], P('sub', None, None, 'grid'), as said below
- coupling_rows: bfloat16 [16, 2048, 256], P('sub', 'grid'), may hold values from -0.09375 to 0.09375
- child_map: int32 [16, 2048], P('sub'), may hold values from 0 to 3071, as said below
Outputs:
- factored: float32 [16, 12, 128, 2, 1536], P('sub', None, None, 'grid')
The draws below stay inside these ranges and needn't reach their ends.
Inputs may be any that keep to these rules, and one draw needn't show every extreme that they name: `child_map`: rows 2 p and 2 p + 1 each hold 2048 distinct indices, and together they name every index of the parent front. `front_entries`: each front is symmetric, and stays positive definite after both children's updates are subtracted.
All inputs are finite; a program needn't handle non-finite values.
Results may differ from the reference program's by a relative error of at most 0.0003.
Values may be sent and summed in bfloat16 or wider, within the bound.
A program may use at most 128 MiB of HBM per device.

```python
import math
import jax
import jax.numpy as jnp
from jax import lax

NB = 128
PF = 3072
SEP = 2048
PIV = 1024
KL = 256
PARENTS = 8
RB = 12
CB = 12
N_SUB = 16
N_GRID = 2


def draw_front_entries(key, part):

    def one_parent(index):
        parent_key = jax.random.fold_in(key, index)
        noise_key, diag_key, sign_key, place_key, size_key = jax.random.split(parent_key, 5)
        spread = 1.6 / math.sqrt(PF)
        raw = spread * jax.random.truncated_normal(noise_key, -6.0, 6.0, (PF, PF), jnp.float32)
        diag = jax.random.uniform(diag_key, (PF,), jnp.float32, 8.0, 12.0)
        signs = 2.0 * jax.random.bernoulli(sign_key, 0.5, (PF,)).astype(jnp.float32) - 1.0
        weight = signs * jax.random.uniform(size_key, (PF,), jnp.float32, 0.5, 1.5)
        places = jax.random.uniform(place_key, (PF,), jnp.float32)
        smooth = 240.0 / PF * weight[:, None] * weight[None, :] * jnp.exp(-jnp.abs(places[:, None] - places[None, :]) / 0.3)
        symmetric = (raw + raw.T) * 0.7071067811865476
        identity = jnp.eye(PF, dtype=bool)
        whole = jnp.where(identity, diag[None, :], symmetric) + smooth
        return whole.reshape(RB, 2, NB, CB, N_GRID, NB).transpose(1, 0, 2, 4, 3, 5).reshape(2, RB, NB, N_GRID, CB * NB)
    output = lax.map(one_parent, jnp.arange(PARENTS, dtype=jnp.int32))
    return output.reshape(N_SUB, RB, NB, N_GRID, CB * NB)


def draw_child_map(key, part):

    def one_parent(index):
        order = jax.random.permutation(jax.random.fold_in(key, index + 7919), PF)
        return jnp.stack([order[:SEP], order[PF - SEP:]], 0)
    output = jax.vmap(one_parent)(jnp.arange(PARENTS, dtype=jnp.int32))
    return output.reshape(N_SUB, SEP).astype(jnp.int32)


def levels(key, dims, pieces, smallest, largest):
    factor_of, own = 1.0, jax.random.fold_in(key, 6)
    for axis_at, parts in pieces:
        draws = jnp.exp(jax.random.uniform(jax.random.fold_in(own, axis_at), (parts,), jnp.float32, smallest / len(pieces), largest / len(pieces)))
        factor_of = factor_of * jnp.repeat(draws, dims[axis_at] // parts).reshape([-1 if axis == axis_at else 1 for axis in range(len(dims))])
    return factor_of


def bell_draw(key, dims, scale, bound, cuts=(), held_as=jnp.bfloat16):
    drawn = scale * jax.random.normal(key, dims, jnp.float32)
    if cuts:
        drawn = drawn * levels(key, dims, cuts, -0.22, 0.18)
    return jnp.clip(drawn, -bound, bound).astype(held_as)


def setup_inputs(seed: int = 0) -> dict:
    seeds = jax.random.split(jax.random.key(seed), 4)
    front_entries = draw_front_entries(jax.random.fold_in(seeds[3], 71), 0)
    coupling_rows = bell_draw(seeds[1], (N_SUB, SEP, KL), (2 * (SEP + KL)) ** -0.5, 0.09375, ((0, 16), (1, 2)))
    child_map = draw_child_map(jax.random.fold_in(seeds[3], 71), 0)
    return dict(front_entries=front_entries, coupling_rows=coupling_rows, child_map=child_map)


def reference(front_entries, coupling_rows, child_map):
    fronts = front_entries.reshape(PARENTS, 2, RB, NB, N_GRID, CB * NB)
    factors = coupling_rows.reshape(PARENTS, 2, SEP, KL)
    mappings = child_map.reshape(PARENTS, 2, SEP)

    def one_parent(items):
        front, factor, mapping = items
        whole = front.reshape(2, RB, NB, N_GRID, CB, NB).transpose(1, 0, 2, 4, 3, 5).reshape(PF, PF)
        for child in range(2):
            update = jnp.dot(factor[child].astype(jnp.float32), factor[child].T.astype(jnp.float32), preferred_element_type=jnp.float32)
            whole = whole.at[mapping[child][:, None], mapping[child][None, :]].add(-update)
        pivot = jnp.tril(jnp.linalg.cholesky(whole[:PIV, :PIV]))
        below = jax.scipy.linalg.solve_triangular(pivot, whole[PIV:, :PIV].T, lower=True).T
        schur = whole[PIV:, PIV:] - jnp.dot(below, below.T, precision=lax.Precision.HIGHEST)
        result = jnp.zeros((PF, PF), jnp.float32)
        result = result.at[:PIV, :PIV].set(pivot).at[PIV:, :PIV].set(below).at[PIV:, PIV:].set(schur)
        return result.reshape(RB, 2, NB, CB, N_GRID, NB).transpose(1, 0, 2, 4, 3, 5).reshape(2, RB, NB, N_GRID, CB * NB)
    output = lax.map(one_parent, (fronts, factors, mappings))
    return output.reshape(N_SUB, RB, NB, N_GRID, CB * NB)
```

```python
import functools

import jax
import jax.numpy as jnp
from jax import lax
from jax.experimental import pallas as pl
from jax.experimental.pallas import tpu as pltpu
from jax.sharding import PartitionSpec as P

NB = 128
PF = 3072
PIV = 1024
NPB = PIV // NB
SUBL = 8
EXTRA = 16
NT = (((1,), (1,)), ((), ()))
NN = (((1,), (0,)), ((), ()))
F32 = jnp.float32
BF16 = jnp.bfloat16


def dot(a, b, dims=NN):
    return lax.dot_general(a, b, dims, preferred_element_type=F32)


def split(x):
    high = x.astype(BF16)
    return high, (x - high.astype(F32)).astype(BF16)


def dot3(a, b, dims=NN):
    ah, al = split(a)
    bh, bl = split(b)
    return dot(ah, bh, dims) + (dot(al, bh, dims) + dot(ah, bl, dims))


def sibling_swap(shard):
    return lax.ppermute(shard, "sub", [(i, i ^ 1) for i in range(lax.axis_size("sub"))])


def ring_gather(shard):
    count = lax.axis_size("grid")
    parts = [shard]
    for k in range(1, count):
        parts.append(lax.ppermute(shard, "grid", [((i + k) % count, i) for i in range(count)]))
    return jnp.stack(parts)


def block(index):
    return pl.ds(pl.multiple_of(index * NB, NB), NB)


def expand_kernel(map_ref, rows_ref, out_ref):
    rows = out_ref.shape[0]
    width = rows_ref.shape[2]
    first = pl.program_id(0) * rows
    for child in range(2):
        ids = first + lax.broadcasted_iota(jnp.int32, (rows, map_ref.shape[2]), 0)
        hot = jnp.where(map_ref[child] == ids, 1.0, 0.0).astype(BF16)
        out_ref[:, child * width : (child + 1) * width] = dot(hot, rows_ref[child]).astype(BF16)


def expand(maps, rows):
    tile = 256
    width = rows.shape[2]
    return pl.pallas_call(
        expand_kernel,
        grid=(PF // tile,),
        in_specs=[
            pl.BlockSpec(maps.shape, lambda i: (0, 0, 0)),
            pl.BlockSpec(rows.shape, lambda i: (0, 0, 0)),
        ],
        out_specs=pl.BlockSpec((tile, 2 * width), lambda i: (i, 0)),
        out_shape=jax.ShapeDtypeStruct((PF, 2 * width), BF16),
        name="expand",
    )(maps, rows)


def factor_block(diag):
    groups = NB // SUBL
    a = [diag[v * SUBL : (v + 1) * SUBL] for v in range(groups)]
    lane = lax.broadcasted_iota(jnp.int32, (SUBL, NB), 1)
    sub = lax.broadcasted_iota(jnp.int32, (SUBL, NB), 0)

    def along(x, row):
        return jnp.broadcast_to(x[row : row + 1], (SUBL, NB))

    for t in range(groups):
        cols = [
            [jnp.broadcast_to(a[v][:, t * SUBL + l : t * SUBL + l + 1], (SUBL, NB)) for l in range(SUBL)]
            for v in range(t, groups)
        ]
        for l in range(SUBL):
            inv_pivot = 1.0 / along(cols[0][l], l)
            row = along(a[t], l) * jnp.where(lane == t * SUBL + l, 2.0, 1.0)
            ahead = [along(cols[0][k], l) for k in range(l + 1, SUBL)]
            for v in range(t, groups):
                mine = cols[v - t]
                m = mine[l] * inv_pivot
                if v == t:
                    m = jnp.where(sub > l, m, 0.0)
                a[v] = a[v] - m * row
                for k in range(l + 1, SUBL):
                    mine[k] = mine[k] - m * ahead[k - l - 1]
    d_lane = jnp.zeros((SUBL, NB), F32)
    on_diag = []
    for v in range(groups):
        on_diag.append(jnp.where(lane == v * SUBL + sub, a[v], 0.0))
        d_lane = d_lane + on_diag[v]
    inv_lane = 1.0 / jnp.sum(d_lane, axis=0, keepdims=True)
    inverse, upper = [], []
    for v in range(groups):
        scale = 1.0 / jnp.sqrt(jnp.sum(on_diag[v], axis=1, keepdims=True))
        at = v * SUBL + sub
        inverse.append(jnp.where(lane <= at, a[v] * inv_lane * scale, 0.0))
        upper.append(jnp.where(lane >= at, a[v] * scale, 0.0))
    return jnp.concatenate(inverse, 0), jnp.concatenate(upper, 0)


def pivot_kernel(grid_count, me_ref, front_ref, rows_ref, factor_ref, high_ref, low_ref, w):
    s, g = me_ref[0], me_ref[1]
    held = front_ref.shape[2] - EXTRA
    eye = lax.broadcasted_iota(jnp.int32, (NB, NB), 0) == lax.broadcasted_iota(jnp.int32, (NB, NB), 1)
    for i in range(NPB):
        at = slice(i * NB, (i + 1) * NB)
        w[at, :] = -dot(rows_ref[at, :], rows_ref[...], NT)
        from_row = lax.rem(i + s, 2)
        for b in range(NPB):
            k = lax.rem(b - g + PIV // NB * grid_count, grid_count)
            cols = slice(b // grid_count * NB, (b // grid_count + 1) * NB)
            there = slice(b * NB, (b + 1) * NB)
            piece = front_ref[from_row, k, i // 2 * NB : (i // 2 + 1) * NB, cols].astype(F32)
            if b == i:
                rest = front_ref[from_row, k, held : held + EXTRA, cols].astype(F32)[:1]
                piece = piece + jnp.where(eye, rest, 0.0)
            w[at, there] += piece

    @pl.loop(0, NPB)
    def _(j):
        at = block(j)
        inverse, upper = factor_block(w[at, at])
        factor_ref[at, at] = upper.T
        w[at, at] = jnp.where(eye, 1.0, 0.0)
        panel = dot3(inverse, w[at, :])
        w[at, :] = panel
        panel16 = panel.astype(BF16)

        @pl.loop(j + 1, NPB)
        def _(i):
            mine = block(i)
            left = w[at, mine].T
            factor_ref[mine, at] = left
            w[mine, at] = jnp.zeros((NB, NB), F32)
            w[mine, :] -= dot(left.astype(BF16), panel16)

    for i in range(NPB):
        at = slice(i * NB, (i + 1) * NB)
        keep = lax.broadcasted_iota(jnp.int32, (NB, PIV), 1) < (i + 1) * NB
        high, low = split(jnp.where(keep, w[at, :], 0.0))
        high_ref[at, :] = high
        low_ref[at, :] = low


def factor_pivots(me, fronts, expanded, grid_count):
    vmem = pl.BlockSpec(memory_space=pltpu.VMEM)
    square = functools.partial(jax.ShapeDtypeStruct, (PIV, PIV))
    return pl.pallas_call(
        functools.partial(pivot_kernel, grid_count),
        grid=(1,),
        in_specs=[
            pl.BlockSpec(memory_space=pltpu.SMEM),
            vmem,
            pl.BlockSpec((PIV, expanded.shape[1]), lambda i: (0, 0)),
        ],
        out_specs=[vmem, vmem, vmem],
        out_shape=[square(F32), square(BF16), square(BF16)],
        scratch_shapes=[pltpu.VMEM((PIV, PIV), F32)],
        cost_estimate=pl.CostEstimate(flops=40 * PIV**3, bytes_accessed=16 * PIV**2, transcendentals=0),
        name="pivots",
    )(me, fronts, expanded)


def schur_kernel(
    grid_count, me_ref, front_ref, left_ref, right_ref, rows_ref, factor_ref, high_ref, low_ref,
    out_ref, mycols, across, xr, xl,
):
    s, g = me_ref[0], me_ref[1]
    r = pl.program_id(0)
    col_blocks = out_ref.shape[0] // NB
    done = NPB // grid_count

    @pl.when(r == 0)
    def _():
        for c in range(col_blocks):
            mycols[c * NB : (c + 1) * NB, :] = rows_ref[block(c * grid_count + g), :]
        for i in range(NPB):
            at = slice(i * NB, (i + 1) * NB)
            piece = right_ref[lax.rem(i + s, 2), i // 2 * NB : (i // 2 + 1) * NB, :].astype(F32)
            across[at, :] = (piece - dot(rows_ref[at, :], mycols[done * NB :, :], NT)).astype(BF16)
        for i in range(NPB):
            at = slice(i * NB, (i + 1) * NB)
            deep = (i + 1) * NB
            xr[at, :] = dot(high_ref[at, :deep], across[:deep, :]).astype(BF16)

    row_id = 2 * r + s

    @pl.when(r < NPB // 2)
    def _():
        for c in range(col_blocks):
            to = pl.ds(c, NB, stride=col_blocks)
            if c < done:
                col_id = c * grid_count + g
                here = factor_ref[block(row_id), block(col_id)]
                out_ref[to, :] = jnp.where(row_id >= col_id, here, 0.0)
            else:
                out_ref[to, :] = jnp.zeros((NB, NB), F32)

    @pl.when(r >= NPB // 2)
    def _():
        mine = rows_ref[block(row_id), :]
        local = block(r - NPB // 2)
        for b in range(NPB):
            k = lax.rem(b - g + NPB * grid_count, grid_count)
            cols = slice(b // grid_count * NB, (b // grid_count + 1) * NB)
            xl[:, b * NB : (b + 1) * NB] = left_ref[k, local, cols].astype(F32)
        a_high, a_low = split(xl[...] - dot(mine, rows_ref[:PIV, :], NT))
        x = dot(a_high, high_ref[...], NT) + (dot(a_low, high_ref[...], NT) + dot(a_high, low_ref[...], NT))
        xl[...] = x
        x16 = x.astype(BF16)
        taken = dot(mine, mycols[done * NB :, :], NT) + dot(x16, xr[...])
        for c in range(col_blocks):
            to = pl.ds(c, NB, stride=col_blocks)
            if c < done:
                out_ref[to, :] = xl[:, block(c * grid_count + g)]
            else:
                out_ref[to, :] = front_ref[to, :] - taken[:, (c - done) * NB : (c - done + 1) * NB]


def schur(me, front, left, right, expanded, factor, high, low, grid_count, col_blocks):
    vmem = pl.BlockSpec(memory_space=pltpu.VMEM)
    tall = NB * col_blocks
    below = (col_blocks - NPB // grid_count) * NB
    return pl.pallas_call(
        functools.partial(schur_kernel, grid_count),
        grid=(front.shape[0] // tall,),
        in_specs=[
            pl.BlockSpec(memory_space=pltpu.SMEM),
            pl.BlockSpec((tall, NB), lambda i: (jnp.maximum(i, NPB // 2), 0)),
        ]
        + [vmem] * 6,
        out_specs=pl.BlockSpec((tall, NB), lambda i: (i, 0)),
        out_shape=jax.ShapeDtypeStruct(front.shape, F32),
        scratch_shapes=[
            pltpu.VMEM((col_blocks * NB, expanded.shape[1]), BF16),
            pltpu.VMEM((PIV, below), BF16),
            pltpu.VMEM((PIV, below), BF16),
            pltpu.VMEM((NB, PIV), F32),
        ],
        compiler_params=pltpu.CompilerParams(vmem_limit_bytes=56 * 1024 * 1024),
        name="schur",
    )(me, front, left, right, expanded, factor, high, low)


def on_device(front_entries, coupling_rows, child_map):
    s = lax.axis_index("sub") % 2
    g = lax.axis_index("grid")
    grid_count = lax.axis_size("grid")
    row_blocks = front_entries.shape[1]
    col_width = front_entries.shape[4]
    col_blocks = col_width // NB
    wide = front_entries.reshape(row_blocks * NB, col_width)
    front = front_entries.reshape(row_blocks * NB * col_blocks, NB)
    me = jnp.stack([s, g]).astype(jnp.int32)
    top, pivot_cols = PIV // 2, PIV // grid_count

    own_rows = ring_gather(coupling_rows[0]).reshape(-1, coupling_rows.shape[2])
    own_map = jnp.roll(child_map[0].reshape(grid_count, -1), -g, axis=0).reshape(1, -1)
    rows = jnp.stack([own_rows, sibling_swap(own_rows)])
    maps = jnp.stack([own_map, sibling_swap(own_map)])

    corner = wide[:top, :pivot_cols]
    rounded = lax.reduce_precision(corner, 8, 7)
    row_ids = (jnp.arange(top, dtype=jnp.int32) // NB * 2 + s) * NB + jnp.arange(top, dtype=jnp.int32) % NB
    spots = jnp.arange(pivot_cols, dtype=jnp.int32)
    col_ids = (spots // NB * grid_count + g) * NB + spots % NB
    rest = jnp.sum(jnp.where(row_ids[:, None] == col_ids[None, :], corner - rounded, 0.0), axis=0)
    piece = jnp.concatenate(
        [corner.astype(BF16), jnp.broadcast_to(rest.astype(BF16)[None], (EXTRA, pivot_cols))]
    )
    held = ring_gather(piece)
    pivots = jnp.stack([held, sibling_swap(held)])
    left = ring_gather(wide[top:, :pivot_cols].astype(BF16))
    over = wide[:top, pivot_cols:].astype(BF16)
    right = jnp.stack([over, sibling_swap(over)])

    expanded = expand(maps, rows)
    factor, high, low = factor_pivots(me, pivots, expanded, grid_count)
    result = schur(me, front, left, right, expanded, factor, high, low, grid_count, col_blocks)
    return result.reshape(front_entries.shape)


MESH = pl.DeviceIdType.MESH
CHUNKS = 4
TILE = 256


def hot_dot(ids, first, rows):
    at = first + lax.broadcasted_iota(jnp.int32, (TILE, ids.shape[1]), 0)
    return dot(jnp.where(ids == at, 1.0, 0.0).astype(BF16), rows)


def exchange_kernel(
    map_ref, rows_ref, front_ref, wide_ref, piv_ref, own_ref, sib_ref,
    rows, maps, front, load, row_send, row_recv, pass_send, pass_recv, near_send, near_recv,
    far_send, far_recv, far_pass_send, far_pass_recv,
):
    sub, g = lax.axis_index("sub"), lax.axis_index("grid")
    s = lax.rem(sub, 2)
    sibling, over = (sub + 1 - 2 * s, g), (sub, 1 - g)
    count, width = rows_ref.shape
    chunk = count // CHUNKS
    col_blocks = front.shape[0] // (piv_ref.shape[1] - EXTRA)
    done = piv_ref.shape[2] // NB
    square = done * NB

    def to(device, src, dst, send, recv):
        return pltpu.make_async_remote_copy(
            src_ref=src, dst_ref=dst, send_sem=send, recv_sem=recv, device_id=device, device_id_type=MESH
        )

    loads = [
        pltpu.make_async_copy(rows_ref, rows.at[s, g], load.at[0]),
        pltpu.make_async_copy(map_ref, maps.at[s], load.at[1]),
        pltpu.make_async_copy(front_ref.at[pl.ds(0, front.shape[0])], front, load.at[2]),
    ]
    for copy in loads:
        copy.start()
    barrier = pltpu.get_barrier_semaphore()
    for device in (sibling, over):
        pl.semaphore_signal(barrier, inc=1, device_id=device, device_id_type=MESH)
    pl.semaphore_wait(barrier, 2)

    pieces = [pl.ds(k * chunk, chunk) for k in range(CHUNKS)]
    row_copies = [
        to(over, rows_ref.at[at], rows.at[s, g, at], row_send.at[k], row_recv.at[k]) for k, at in enumerate(pieces)
    ]
    row_passes = [
        to(sibling, rows.at[s, 1 - g, at], rows.at[s, 1 - g, at], pass_send.at[k], pass_recv.at[k])
        for k, at in enumerate(pieces)
    ]
    near = [
        to(sibling, rows_ref, rows.at[s, g], near_send.at[0], near_recv.at[0]),
        to(sibling, map_ref, maps.at[s], near_send.at[1], near_recv.at[1]),
        to(sibling, piv_ref.at[s], piv_ref.at[s], near_send.at[2], near_recv.at[2]),
        to(sibling, own_ref, sib_ref, near_send.at[3], near_recv.at[3]),
    ]
    strips = [(pl.ds(r * NB, NB), pl.ds(r * NB, square - r * NB)) for r in range(done)]
    strips.append((pl.ds(square, EXTRA), pl.ds(0, square)))
    far_copies = [
        to(over, piv_ref.at[s, a, b], piv_ref.at[2, a, b], far_send.at[k], far_recv.at[k])
        for k, (a, b) in enumerate(strips)
    ]
    far_passes = [
        to(sibling, piv_ref.at[2, a, b], piv_ref.at[2, a, b], far_pass_send.at[k], far_pass_recv.at[k])
        for k, (a, b) in enumerate(strips)
    ]
    for copy in row_copies:
        copy.start()
    near[0].start()
    near[1].start()

    loads[2].wait()
    eye = lax.broadcasted_iota(jnp.int32, (NB, NB), 0) == lax.broadcasted_iota(jnp.int32, (NB, NB), 1)
    for r in range(done):
        at = slice(r * NB, (r + 1) * NB)
        for c in range(done):
            block_rc = front[pl.ds(r * NB * col_blocks + c, NB, stride=col_blocks), :]
            rounded = block_rc.astype(BF16)
            piv_ref[s, at, c * NB : (c + 1) * NB] = rounded
            if r == c:
                rest = jnp.where(eye, block_rc - rounded.astype(F32), 0.0)
                rest = jnp.broadcast_to(jnp.sum(rest, axis=0, keepdims=True), (EXTRA, NB))
                piv_ref[s, square : square + EXTRA, c * NB : (c + 1) * NB] = rest.astype(BF16)
    near[2].start()

    @pl.when(s == g)
    def _():
        for copy in far_copies:
            copy.start()

    for r in range(done):
        at = slice(r * NB, (r + 1) * NB)
        for c in range(done, col_blocks):
            block_rc = front[pl.ds(r * NB * col_blocks + c, NB, stride=col_blocks), :]
            own_ref[at, (c - done) * NB : (c - done + 1) * NB] = block_rc.astype(BF16)
    near[3].start()

    def spread(child, half, first, size, fresh):
        ids = maps[child, :, pl.ds(pl.multiple_of(half * count + first, NB), size)]
        data = rows[child, half, pl.ds(first, size), :]
        cols = pl.ds(pl.multiple_of(child * width, NB), width)

        @pl.loop(0, wide_ref.shape[0] // TILE)
        def _(t):
            at = pl.ds(pl.multiple_of(t * TILE, TILE), TILE)
            part = hot_dot(ids, t * TILE, data)
            if not fresh:
                part = part + wide_ref[at, cols].astype(F32)
            wide_ref[at, cols] = part.astype(BF16)

    loads[0].wait()
    loads[1].wait()
    spread(s, g, 0, count, True)
    near[0].wait_recv()
    near[1].wait_recv()
    spread(1 - s, g, 0, count, True)
    for k in range(CHUNKS):
        row_copies[k].wait_recv()
        row_passes[k].start()
        spread(s, 1 - g, k * chunk, chunk, False)
        row_passes[k].wait_recv()
        spread(1 - s, 1 - g, k * chunk, chunk, False)

    @pl.when(s == g)
    def _():
        for copy in far_passes:
            copy.wait_recv()
        for copy in far_copies:
            copy.wait_send()

    @pl.when(s != g)
    def _():
        for copy, passed in zip(far_copies, far_passes):
            copy.wait_recv()
            passed.start()
        for passed in far_passes:
            passed.wait_send()

    near[2].wait_recv()
    near[3].wait_recv()
    for copy in near + row_copies + row_passes:
        copy.wait_send()


def exchange(child_map, rows, front, col_blocks):
    vmem = pl.BlockSpec(memory_space=pltpu.VMEM)
    anywhere = pl.BlockSpec(memory_space=pl.ANY)
    top, square = PIV // 2, PIV // 2
    below = col_blocks * NB - square
    count, width = rows.shape
    dma = pltpu.SemaphoreType.DMA
    return pl.pallas_call(
        exchange_kernel,
        in_specs=[anywhere] * 3,
        out_specs=[vmem] * 4,
        out_shape=[
            jax.ShapeDtypeStruct((PF, 2 * width), BF16),
            jax.ShapeDtypeStruct((3, top + EXTRA, square), BF16),
            jax.ShapeDtypeStruct((top, below), BF16),
            jax.ShapeDtypeStruct((top, below), BF16),
        ],
        scratch_shapes=[
            pltpu.VMEM((2, 2, count, width), BF16),
            pltpu.VMEM((2, 1, child_map.shape[1]), jnp.int32),
            pltpu.VMEM((top * col_blocks, NB), F32),
            dma((3,)),
            dma((CHUNKS,)), dma((CHUNKS,)), dma((CHUNKS,)), dma((CHUNKS,)),
            dma((4,)), dma((4,)),
            dma((PIV // 2 // NB + 1,)), dma((PIV // 2 // NB + 1,)),
            dma((PIV // 2 // NB + 1,)), dma((PIV // 2 // NB + 1,)),
        ],
        compiler_params=pltpu.CompilerParams(
            collective_id=0, has_side_effects=True, vmem_limit_bytes=40 * 1024 * 1024
        ),
        name="exchange",
    )(child_map, rows, front)


def paired_pivot_kernel(me_ref, front_ref, rows_ref, factor_ref, high_ref, low_ref, w):
    g = me_ref[1]
    held = front_ref.shape[1] - EXTRA
    eye = lax.broadcasted_iota(jnp.int32, (NB, NB), 0) == lax.broadcasted_iota(jnp.int32, (NB, NB), 1)
    for i in range(NPB):
        at = slice(i * NB, (i + 1) * NB)
        w[at, i * NB :] = -dot(rows_ref[at, :], rows_ref[i * NB :, :], NT)
        for b in range(i, NPB):
            up = slice(i // 2 * NB, i // 2 * NB + NB), slice(b // 2 * NB, b // 2 * NB + NB)
            down = up[1], up[0]
            there = slice(b * NB, (b + 1) * NB)
            if i % 2 == b % 2:
                k = jnp.where(g == i % 2, i % 2, 2)
                piece = front_ref[k, up[0], up[1]].astype(F32)
                if b == i:
                    rest = front_ref[k, held : held + EXTRA, up[1]].astype(F32)[:1]
                    piece = piece + jnp.where(eye, rest, 0.0)
            else:
                direct = front_ref[i % 2, up[0], up[1]].astype(F32)
                mirrored = front_ref[b % 2, down[0], down[1]].astype(F32).T
                piece = jnp.where(g == b % 2, direct, mirrored)
            w[at, there] += piece

    @pl.loop(0, NPB)
    def _(j):
        at = block(j)
        inverse, upper = factor_block(w[at, at])
        factor_ref[at, at] = upper.T
        w[at, at] = jnp.where(eye, 1.0, 0.0)
        panel = dot3(inverse, w[at, :])
        w[at, :] = panel
        panel16 = panel.astype(BF16)

        @pl.loop(j + 1, NPB)
        def _(i):
            mine = block(i)
            left = w[at, mine].T
            factor_ref[mine, at] = left
            w[mine, at] = jnp.zeros((NB, NB), F32)
            w[mine, :] -= dot(left.astype(BF16), panel16)

    for i in range(NPB):
        at = slice(i * NB, (i + 1) * NB)
        keep = lax.broadcasted_iota(jnp.int32, (NB, PIV), 1) < (i + 1) * NB
        high, low = split(jnp.where(keep, w[at, :], 0.0))
        high_ref[at, :] = high
        low_ref[at, :] = low


def paired_pivots(me, fronts, expanded):
    vmem = pl.BlockSpec(memory_space=pltpu.VMEM)
    square = functools.partial(jax.ShapeDtypeStruct, (PIV, PIV))
    return pl.pallas_call(
        paired_pivot_kernel,
        grid=(1,),
        in_specs=[
            pl.BlockSpec(memory_space=pltpu.SMEM),
            vmem,
            pl.BlockSpec((PIV, expanded.shape[1]), lambda i: (0, 0)),
        ],
        out_specs=[vmem, vmem, vmem],
        out_shape=[square(F32), square(BF16), square(BF16)],
        scratch_shapes=[pltpu.VMEM((PIV, PIV), F32)],
        cost_estimate=pl.CostEstimate(flops=40 * PIV**3, bytes_accessed=16 * PIV**2, transcendentals=0),
        name="pivots",
    )(me, fronts, expanded)


def paired_schur_kernel(
    me_ref, front_ref, own_ref, sib_ref, far_ref, rows_ref, factor_ref, high_ref, low_ref,
    out_ref, mycols, across, xr, other, xl,
):
    s, g = me_ref[0], me_ref[1]
    step = pl.program_id(0)
    below = own_ref.shape[1]
    half = PIV // 2
    done = half // NB
    col_blocks = done + below // NB
    per = out_ref.shape[0] // (NB * col_blocks)
    tall = per * NB
    pivot_steps = done // per

    @pl.when(step == 0)
    def _():
        for c in range(below // NB):
            mycols[c * NB : (c + 1) * NB, :] = rows_ref[block((c + done) * 2 + g), :]
        for i in range(done):
            at = slice(i * NB, (i + 1) * NB)
            both = slice(2 * i * NB, 2 * (i + 1) * NB)
            here, there = own_ref[at, :].astype(F32), sib_ref[at, :].astype(F32)
            piece = jnp.concatenate([jnp.where(s == 0, here, there), jnp.where(s == 0, there, here)], 0)
            across[both, :] = (piece - dot(rows_ref[both, :], mycols[...], NT)).astype(BF16)
            other[:, at] = jnp.where(s == g, there, far_ref[at, :].astype(F32)).T.astype(BF16)

    @pl.when(step == 1)
    def _():
        for i in range(done):
            both = slice(2 * i * NB, 2 * (i + 1) * NB)
            deep = 2 * (i + 1) * NB
            xr[both, :] = dot(high_ref[both, :deep], across[:deep, :]).astype(BF16)

    @pl.when(step < pivot_steps)
    def _():
        for p in range(per):
            row_id = 2 * (step * per + p) + s
            for c in range(col_blocks):
                to = pl.ds(p * NB * col_blocks + c, NB, stride=col_blocks)
                if c < done:
                    col_id = 2 * c + g
                    here = factor_ref[block(row_id), block(col_id)]
                    out_ref[to, :] = jnp.where(row_id >= col_id, here, 0.0)
                else:
                    out_ref[to, :] = jnp.zeros((NB, NB), F32)

    @pl.when(step >= pivot_steps)
    def _():
        mine = jnp.concatenate([rows_ref[block(2 * (step * per + p) + s), :] for p in range(per)], 0)
        local = pl.ds(pl.multiple_of((step - pivot_steps) * tall, tall), tall)
        for c in range(done):
            for p in range(per):
                piece = front_ref[pl.ds(p * NB * col_blocks + c, NB, stride=col_blocks), :]
                xl[p * NB : (p + 1) * NB, block(2 * c + g)] = piece
            xl[:, block(2 * c + 1 - g)] = other[local, c * NB : (c + 1) * NB].astype(F32)
        a_high, a_low = split(xl[...] - dot(mine, rows_ref[:PIV, :], NT))
        for i in range(done):
            both = slice(2 * i * NB, 2 * (i + 1) * NB)
            deep = 2 * (i + 1) * NB
            l_high, l_low = high_ref[both, :deep], low_ref[both, :deep]
            xl[:, both] = dot(a_high[:, :deep], l_high, NT) + (
                dot(a_low[:, :deep], l_high, NT) + dot(a_high[:, :deep], l_low, NT)
            )
        taken = dot(mine, mycols[...], NT) + dot(xl[...].astype(BF16), xr[...])
        for p in range(per):
            at = slice(p * NB, (p + 1) * NB)
            for c in range(col_blocks):
                to = pl.ds(p * NB * col_blocks + c, NB, stride=col_blocks)
                if c < done:
                    out_ref[to, :] = xl[at, block(2 * c + g)]
                else:
                    out_ref[to, :] = front_ref[to, :] - taken[at, (c - done) * NB : (c - done + 1) * NB]


def paired_schur(me, front, own, sib, far, expanded, factor, high, low, col_blocks):
    vmem = pl.BlockSpec(memory_space=pltpu.VMEM)
    per = 2
    tall = per * NB * col_blocks
    first = PIV // 2 // NB // per
    below = own.shape[1]
    tall_below = front.shape[0] // col_blocks - PIV // 2
    return pl.pallas_call(
        paired_schur_kernel,
        grid=(front.shape[0] // tall,),
        in_specs=[
            pl.BlockSpec(memory_space=pltpu.SMEM),
            pl.BlockSpec((tall, NB), lambda i: (jnp.maximum(i, first), 0)),
        ]
        + [vmem] * 7,
        out_specs=pl.BlockSpec((tall, NB), lambda i: (i, 0)),
        out_shape=jax.ShapeDtypeStruct(front.shape, F32),
        scratch_shapes=[
            pltpu.VMEM((below, expanded.shape[1]), BF16),
            pltpu.VMEM((PIV, below), BF16),
            pltpu.VMEM((PIV, below), BF16),
            pltpu.VMEM((tall_below, PIV // 2), BF16),
            pltpu.VMEM((per * NB, PIV), F32),
        ],
        compiler_params=pltpu.CompilerParams(vmem_limit_bytes=48 * 1024 * 1024),
        name="schur",
    )(me, front, own, sib, far, expanded, factor, high, low)


def paired_device(front_entries, coupling_rows, child_map):
    s = lax.axis_index("sub") % 2
    g = lax.axis_index("grid")
    row_blocks, _, _, col_width = front_entries.shape[1:]
    col_blocks = col_width // NB
    front = front_entries.reshape(row_blocks * NB * col_blocks, NB)
    me = jnp.stack([s, g]).astype(jnp.int32)
    expanded, fronts, own, sib = exchange(child_map, coupling_rows[0], front, col_blocks)
    pairs = [(2 * i + i % 2, 2 * i + 1 - i % 2) for i in range(lax.axis_size("sub"))]
    far = lax.ppermute(own, ("sub", "grid"), pairs)
    factor, high, low = paired_pivots(me, fronts, expanded)
    result = paired_schur(me, front, own, sib, far, expanded, factor, high, low, col_blocks)
    return result.reshape(front_entries.shape)


def solution(mesh):
    return jax.shard_map(
        paired_device if mesh.shape["grid"] == 2 else on_device,
        mesh=mesh,
        in_specs=(P("sub", None, None, "grid", None), P("sub", "grid", None), P("sub", None)),
        out_specs=P("sub", None, None, "grid", None),
        check_vma=False,
    )
```

```python
import functools

import jax
import jax.numpy as jnp
from jax import lax
from jax.experimental import pallas as pl
from jax.experimental.pallas import tpu as pltpu
from jax.sharding import PartitionSpec as P

NB = 128
PF = 3072
PIV = 1024
NPB = PIV // NB
SUBL = 8
EXTRA = 16
NT = (((1,), (1,)), ((), ()))
NN = (((1,), (0,)), ((), ()))
F32 = jnp.float32
BF16 = jnp.bfloat16


def dot(a, b, dims=NN):
    return lax.dot_general(a, b, dims, preferred_element_type=F32)


def split(x):
    high = x.astype(BF16)
    return high, (x - high.astype(F32)).astype(BF16)


def dot3(a, b, dims=NN):
    ah, al = split(a)
    bh, bl = split(b)
    return dot(ah, bh, dims) + (dot(al, bh, dims) + dot(ah, bl, dims))


def sibling_swap(shard):
    return lax.ppermute(shard, "sub", [(i, i ^ 1) for i in range(lax.axis_size("sub"))])


def ring_gather(shard):
    count = lax.axis_size("grid")
    parts = [shard]
    for k in range(1, count):
        parts.append(lax.ppermute(shard, "grid", [((i + k) % count, i) for i in range(count)]))
    return jnp.stack(parts)


def block(index):
    return pl.ds(pl.multiple_of(index * NB, NB), NB)


def expand_kernel(map_ref, rows_ref, out_ref):
    rows = out_ref.shape[0]
    width = rows_ref.shape[2]
    first = pl.program_id(0) * rows
    for child in range(2):
        ids = first + lax.broadcasted_iota(jnp.int32, (rows, map_ref.shape[2]), 0)
        hot = jnp.where(map_ref[child] == ids, 1.0, 0.0).astype(BF16)
        out_ref[:, child * width : (child + 1) * width] = dot(hot, rows_ref[child]).astype(BF16)


def expand(maps, rows):
    tile = 256
    width = rows.shape[2]
    return pl.pallas_call(
        expand_kernel,
        grid=(PF // tile,),
        in_specs=[
            pl.BlockSpec(maps.shape, lambda i: (0, 0, 0)),
            pl.BlockSpec(rows.shape, lambda i: (0, 0, 0)),
        ],
        out_specs=pl.BlockSpec((tile, 2 * width), lambda i: (i, 0)),
        out_shape=jax.ShapeDtypeStruct((PF, 2 * width), BF16),
        name="expand",
    )(maps, rows)


def factor_block(diag):
    groups = NB // SUBL
    a = [diag[v * SUBL : (v + 1) * SUBL] for v in range(groups)]
    lane = lax.broadcasted_iota(jnp.int32, (SUBL, NB), 1)
    sub = lax.broadcasted_iota(jnp.int32, (SUBL, NB), 0)

    def along(x, row):
        return jnp.broadcast_to(x[row : row + 1], (SUBL, NB))

    for t in range(groups):
        cols = [
            [jnp.broadcast_to(a[v][:, t * SUBL + l : t * SUBL + l + 1], (SUBL, NB)) for l in range(SUBL)]
            for v in range(t, groups)
        ]
        for l in range(SUBL):
            inv_pivot = 1.0 / along(cols[0][l], l)
            row = along(a[t], l) * jnp.where(lane == t * SUBL + l, 2.0, 1.0)
            ahead = [along(cols[0][k], l) for k in range(l + 1, SUBL)]
            for v in range(t, groups):
                mine = cols[v - t]
                m = mine[l] * inv_pivot
                if v == t:
                    m = jnp.where(sub > l, m, 0.0)
                a[v] = a[v] - m * row
                for k in range(l + 1, SUBL):
                    mine[k] = mine[k] - m * ahead[k - l - 1]
    d_lane = jnp.zeros((SUBL, NB), F32)
    on_diag = []
    for v in range(groups):
        on_diag.append(jnp.where(lane == v * SUBL + sub, a[v], 0.0))
        d_lane = d_lane + on_diag[v]
    inv_lane = 1.0 / jnp.sum(d_lane, axis=0, keepdims=True)
    inverse, upper = [], []
    for v in range(groups):
        scale = 1.0 / jnp.sqrt(jnp.sum(on_diag[v], axis=1, keepdims=True))
        at = v * SUBL + sub
        inverse.append(jnp.where(lane <= at, a[v] * inv_lane * scale, 0.0))
        upper.append(jnp.where(lane >= at, a[v] * scale, 0.0))
    return jnp.concatenate(inverse, 0), jnp.concatenate(upper, 0)


def pivot_kernel(grid_count, me_ref, front_ref, rows_ref, factor_ref, high_ref, low_ref, w):
    s, g = me_ref[0], me_ref[1]
    held = front_ref.shape[2] - EXTRA
    eye = lax.broadcasted_iota(jnp.int32, (NB, NB), 0) == lax.broadcasted_iota(jnp.int32, (NB, NB), 1)
    for i in range(NPB):
        at = slice(i * NB, (i + 1) * NB)
        w[at, :] = -dot(rows_ref[at, :], rows_ref[...], NT)
        from_row = lax.rem(i + s, 2)
        for b in range(NPB):
            k = lax.rem(b - g + PIV // NB * grid_count, grid_count)
            cols = slice(b // grid_count * NB, (b // grid_count + 1) * NB)
            there = slice(b * NB, (b + 1) * NB)
            piece = front_ref[from_row, k, i // 2 * NB : (i // 2 + 1) * NB, cols].astype(F32)
            if b == i:
                rest = front_ref[from_row, k, held : held + EXTRA, cols].astype(F32)[:1]
                piece = piece + jnp.where(eye, rest, 0.0)
            w[at, there] += piece

    @pl.loop(0, NPB)
    def _(j):
        at = block(j)
        inverse, upper = factor_block(w[at, at])
        factor_ref[at, at] = upper.T
        w[at, at] = jnp.where(eye, 1.0, 0.0)
        panel = dot3(inverse, w[at, :])
        w[at, :] = panel
        panel16 = panel.astype(BF16)

        @pl.loop(j + 1, NPB)
        def _(i):
            mine = block(i)
            left = w[at, mine].T
            factor_ref[mine, at] = left
            w[mine, at] = jnp.zeros((NB, NB), F32)
            w[mine, :] -= dot(left.astype(BF16), panel16)

    for i in range(NPB):
        at = slice(i * NB, (i + 1) * NB)
        keep = lax.broadcasted_iota(jnp.int32, (NB, PIV), 1) < (i + 1) * NB
        high, low = split(jnp.where(keep, w[at, :], 0.0))
        high_ref[at, :] = high
        low_ref[at, :] = low


def factor_pivots(me, fronts, expanded, grid_count):
    vmem = pl.BlockSpec(memory_space=pltpu.VMEM)
    square = functools.partial(jax.ShapeDtypeStruct, (PIV, PIV))
    return pl.pallas_call(
        functools.partial(pivot_kernel, grid_count),
        grid=(1,),
        in_specs=[
            pl.BlockSpec(memory_space=pltpu.SMEM),
            vmem,
            pl.BlockSpec((PIV, expanded.shape[1]), lambda i: (0, 0)),
        ],
        out_specs=[vmem, vmem, vmem],
        out_shape=[square(F32), square(BF16), square(BF16)],
        scratch_shapes=[pltpu.VMEM((PIV, PIV), F32)],
        cost_estimate=pl.CostEstimate(flops=40 * PIV**3, bytes_accessed=16 * PIV**2, transcendentals=0),
        name="pivots",
    )(me, fronts, expanded)


def schur_kernel(
    grid_count, me_ref, front_ref, left_ref, right_ref, rows_ref, factor_ref, high_ref, low_ref,
    out_ref, mycols, across, xr, xl,
):
    s, g = me_ref[0], me_ref[1]
    r = pl.program_id(0)
    col_blocks = out_ref.shape[0] // NB
    done = NPB // grid_count

    @pl.when(r == 0)
    def _():
        for c in range(col_blocks):
            mycols[c * NB : (c + 1) * NB, :] = rows_ref[block(c * grid_count + g), :]
        for i in range(NPB):
            at = slice(i * NB, (i + 1) * NB)
            piece = right_ref[lax.rem(i + s, 2), i // 2 * NB : (i // 2 + 1) * NB, :].astype(F32)
            across[at, :] = (piece - dot(rows_ref[at, :], mycols[done * NB :, :], NT)).astype(BF16)
        for i in range(NPB):
            at = slice(i * NB, (i + 1) * NB)
            deep = (i + 1) * NB
            xr[at, :] = dot(high_ref[at, :deep], across[:deep, :]).astype(BF16)

    row_id = 2 * r + s

    @pl.when(r < NPB // 2)
    def _():
        for c in range(col_blocks):
            to = pl.ds(c, NB, stride=col_blocks)
            if c < done:
                col_id = c * grid_count + g
                here = factor_ref[block(row_id), block(col_id)]
                out_ref[to, :] = jnp.where(row_id >= col_id, here, 0.0)
            else:
                out_ref[to, :] = jnp.zeros((NB, NB), F32)

    @pl.when(r >= NPB // 2)
    def _():
        mine = rows_ref[block(row_id), :]
        local = block(r - NPB // 2)
        for b in range(NPB):
            k = lax.rem(b - g + NPB * grid_count, grid_count)
            cols = slice(b // grid_count * NB, (b // grid_count + 1) * NB)
            xl[:, b * NB : (b + 1) * NB] = left_ref[k, local, cols].astype(F32)
        a_high, a_low = split(xl[...] - dot(mine, rows_ref[:PIV, :], NT))
        x = dot(a_high, high_ref[...], NT) + (dot(a_low, high_ref[...], NT) + dot(a_high, low_ref[...], NT))
        xl[...] = x
        x16 = x.astype(BF16)
        taken = dot(mine, mycols[done * NB :, :], NT) + dot(x16, xr[...])
        for c in range(col_blocks):
            to = pl.ds(c, NB, stride=col_blocks)
            if c < done:
                out_ref[to, :] = xl[:, block(c * grid_count + g)]
            else:
                out_ref[to, :] = front_ref[to, :] - taken[:, (c - done) * NB : (c - done + 1) * NB]


def schur(me, front, left, right, expanded, factor, high, low, grid_count, col_blocks):
    vmem = pl.BlockSpec(memory_space=pltpu.VMEM)
    tall = NB * col_blocks
    below = (col_blocks - NPB // grid_count) * NB
    return pl.pallas_call(
        functools.partial(schur_kernel, grid_count),
        grid=(front.shape[0] // tall,),
        in_specs=[
            pl.BlockSpec(memory_space=pltpu.SMEM),
            pl.BlockSpec((tall, NB), lambda i: (jnp.maximum(i, NPB // 2), 0)),
        ]
        + [vmem] * 6,
        out_specs=pl.BlockSpec((tall, NB), lambda i: (i, 0)),
        out_shape=jax.ShapeDtypeStruct(front.shape, F32),
        scratch_shapes=[
            pltpu.VMEM((col_blocks * NB, expanded.shape[1]), BF16),
            pltpu.VMEM((PIV, below), BF16),
            pltpu.VMEM((PIV, below), BF16),
            pltpu.VMEM((NB, PIV), F32),
        ],
        compiler_params=pltpu.CompilerParams(vmem_limit_bytes=56 * 1024 * 1024),
        name="schur",
    )(me, front, left, right, expanded, factor, high, low)


def on_device(front_entries, coupling_rows, child_map):
    s = lax.axis_index("sub") % 2
    g = lax.axis_index("grid")
    grid_count = lax.axis_size("grid")
    row_blocks = front_entries.shape[1]
    col_width = front_entries.shape[4]
    col_blocks = col_width // NB
    wide = front_entries.reshape(row_blocks * NB, col_width)
    front = front_entries.reshape(row_blocks * NB * col_blocks, NB)
    me = jnp.stack([s, g]).astype(jnp.int32)
    top, pivot_cols = PIV // 2, PIV // grid_count

    own_rows = ring_gather(coupling_rows[0]).reshape(-1, coupling_rows.shape[2])
    own_map = jnp.roll(child_map[0].reshape(grid_count, -1), -g, axis=0).reshape(1, -1)
    rows = jnp.stack([own_rows, sibling_swap(own_rows)])
    maps = jnp.stack([own_map, sibling_swap(own_map)])

    corner = wide[:top, :pivot_cols]
    rounded = lax.reduce_precision(corner, 8, 7)
    row_ids = (jnp.arange(top, dtype=jnp.int32) // NB * 2 + s) * NB + jnp.arange(top, dtype=jnp.int32) % NB
    spots = jnp.arange(pivot_cols, dtype=jnp.int32)
    col_ids = (spots // NB * grid_count + g) * NB + spots % NB
    rest = jnp.sum(jnp.where(row_ids[:, None] == col_ids[None, :], corner - rounded, 0.0), axis=0)
    piece = jnp.concatenate(
        [corner.astype(BF16), jnp.broadcast_to(rest.astype(BF16)[None], (EXTRA, pivot_cols))]
    )
    held = ring_gather(piece)
    pivots = jnp.stack([held, sibling_swap(held)])
    left = ring_gather(wide[top:, :pivot_cols].astype(BF16))
    over = wide[:top, pivot_cols:].astype(BF16)
    right = jnp.stack([over, sibling_swap(over)])

    expanded = expand(maps, rows)
    factor, high, low = factor_pivots(me, pivots, expanded, grid_count)
    result = schur(me, front, left, right, expanded, factor, high, low, grid_count, col_blocks)
    return result.reshape(front_entries.shape)


MESH = pl.DeviceIdType.MESH
CHUNKS = 4
TILE = 1024


SUPER = 32
TN = (((0,), (0,)), ((), ()))


def factor_pieces(diag):
    groups = NB // SUBL
    per = SUPER // SUBL
    a = [diag[v * SUBL : (v + 1) * SUBL] for v in range(groups)]
    lane = lax.broadcasted_iota(jnp.int32, (SUBL, NB), 1)
    sub = lax.broadcasted_iota(jnp.int32, (SUBL, NB), 0)

    def along(x, row):
        return jnp.broadcast_to(x[row : row + 1], (SUBL, NB))

    zero = lax.shift_right_logical(lane, 8).astype(F32)

    def columns(rows, t):
        out = [[None] * SUBL for _ in rows]
        for l in range(SUBL):
            for n, v in enumerate(rows):
                at = t * SUBL + l
                out[n][l] = jnp.broadcast_to(a[v][:, at : at + 1], (SUBL, NB)) + zero
        return out

    inverses = []
    for start in range(0, groups, per):
        stop = start + per
        ready = columns(range(start, stop), start)
        for t in range(start, stop):
            mine = ready
            ready = columns(range(t + 1, stop), t + 1) if t + 1 < stop else []
            by_row = jnp.zeros((SUBL, NB), F32)
            for l in range(SUBL):
                inv_pivot = 1.0 / along(mine[0][l], l)
                by_row = jnp.where(sub == l, inv_pivot, by_row)
                row = along(a[t], l) * jnp.where(lane == t * SUBL + l, 2.0, 1.0)
                ahead = [along(mine[0][k], l) for k in range(l + 1, SUBL)]
                beyond = [along(mine[1][l], k) for k in range(SUBL)] if t + 1 < stop else []
                for v in range(t, stop):
                    at = mine[v - t]
                    m = at[l] * inv_pivot
                    for k in range(l + 1, SUBL):
                        at[k] = at[k] - m * ahead[k - l - 1]
                    if v > t:
                        later = ready[v - t - 1]
                        for k in range(SUBL):
                            later[k] = later[k] - m * beyond[k]
                    else:
                        m = jnp.where(sub > l, m, 0.0)
                    a[v] = a[v] - m * row
            inverses.append(by_row)
        if stop < groups:
            left = jnp.concatenate([a[v] * inverses[v] for v in range(start, stop)], 0)
            inside = (lane >= start * SUBL) & (lane < stop * SUBL)
            right = jnp.concatenate(
                [jnp.where(inside & (lane > v * SUBL + sub), 0.0, a[v]) for v in range(start, stop)], 0
            )
            change = dot(left.astype(BF16), right.astype(BF16), TN)
            for v in range(stop, groups):
                a[v] = jnp.where(inside, 0.0, a[v]) - change[v * SUBL : (v + 1) * SUBL]
    d_lane = jnp.zeros((SUBL, NB), F32)
    for v in range(groups):
        d_lane = d_lane + jnp.where(lane == v * SUBL + sub, inverses[v], 0.0)
    inv_lane = jnp.sum(d_lane, axis=0, keepdims=True)
    inverse, upper = [], []
    for v in range(groups):
        scale = jnp.sqrt(inverses[v])
        at = v * SUBL + sub
        inverse.append(jnp.where(lane <= at, a[v] * inv_lane * scale, 0.0))
        upper.append(jnp.where(lane >= at, a[v] * scale, 0.0))
    return jnp.concatenate(inverse, 0), jnp.concatenate(upper, 0)


def factor_pivots_paired(g, front_ref, rows_ref, factor_ref, high_ref, low_ref, upper_ref, held, gone):
    rest_at = front_ref.shape[1] - EXTRA
    eye = lax.broadcasted_iota(jnp.int32, (NB, NB), 0) == lax.broadcasted_iota(jnp.int32, (NB, NB), 1)
    for i in range(NPB):
        at = slice(i * NB, (i + 1) * NB)
        held[at, :] = jnp.zeros((NB, PIV), BF16)
        if i:
            factor_ref[at, : i * NB] = jnp.zeros((NB, i * NB), F32)
        update = dot(rows_ref[at, :], rows_ref[i * NB : PIV, :], NT)
        for b in range(i, NPB):
            up = slice(i // 2 * NB, i // 2 * NB + NB), slice(b // 2 * NB, b // 2 * NB + NB)
            down = up[1], up[0]
            if i % 2 == b % 2:
                k = 2 - (2 - i % 2) * (1 - g - i % 2 + 2 * g * (i % 2))
                piece = front_ref[k, up[0], up[1]].astype(F32)
                if b == i:
                    rest = front_ref[k, rest_at : rest_at + EXTRA, up[1]].astype(F32)[:1]
                    piece = piece + jnp.where(eye, rest, 0.0)
            else:
                direct = front_ref[i % 2, up[0], up[1]].astype(F32)
                mirrored = front_ref[b % 2, down[0], down[1]].astype(F32).T
                piece = jnp.where(g == b % 2, direct, mirrored)
            factor_ref[at, b * NB : (b + 1) * NB] = piece - update[:, (b - i) * NB : (b - i + 1) * NB]

    lane = lax.broadcasted_iota(jnp.int32, (NB, PIV), 1)

    @pl.loop(0, NPB)
    def _(j):
        at, after = block(j), block(lax.rem(j + 1, NPB))
        held[:, at] = jnp.zeros((PIV, NB), BF16)
        gone[...] = dot(held[:, after], held[...], TN)
        inverse, upper = factor_pieces(factor_ref[at, at])
        upper_ref[at, :] = upper
        factor_ref[at, at] = jnp.where(eye, 1.0, 0.0)
        panel = dot3(inverse, factor_ref[at, :])
        factor_ref[at, :] = panel
        panel16 = panel.astype(BF16)
        held[at, :] = panel16
        high, low = split(jnp.where(lane < (j + 1) * NB, panel, 0.0))
        high_ref[at, :] = high
        low_ref[at, :] = low

        @pl.when(j < NPB - 1)
        def _():
            factor_ref[after, :] = factor_ref[after, :] - gone[...] - dot(held[at, after], panel16, TN)


def hot_dot(ids, first, rows):
    at = first + lax.broadcasted_iota(jnp.int32, (TILE, ids.shape[1]), 0)
    return dot(jnp.where(ids == at, 1.0, 0.0).astype(BF16), rows)


def exchange_kernel(
    map_ref, rows_ref, front_ref, wide_ref, own_ref, sib_ref, far_ref, factor_ref, high_ref, low_ref, upper_ref,
    rows, maps, front, piv_ref, held, gone, load, row_send, row_recv, pass_send, pass_recv, near_send, near_recv,
    far_send, far_recv, far_pass_send, far_pass_recv, panel_send, panel_recv,
):
    sub, g = lax.axis_index("sub"), lax.axis_index("grid")
    s = lax.rem(sub, 2)
    sibling, over = (sub + 1 - 2 * s, g), (sub, 1 - g)
    count, width = rows_ref.shape
    chunk = count // CHUNKS
    col_blocks = front.shape[0] // (piv_ref.shape[1] - EXTRA)
    done = piv_ref.shape[2] // NB
    square = done * NB

    def to(device, src, dst, send, recv):
        return pltpu.make_async_remote_copy(
            src_ref=src, dst_ref=dst, send_sem=send, recv_sem=recv, device_id=device, device_id_type=MESH
        )

    loads = [
        pltpu.make_async_copy(rows_ref, rows.at[s, g], load.at[0]),
        pltpu.make_async_copy(map_ref, maps.at[s], load.at[1]),
        pltpu.make_async_copy(front_ref.at[pl.ds(0, front.shape[0])], front, load.at[2]),
    ]
    for copy in loads:
        copy.start()
    barrier = pltpu.get_barrier_semaphore()
    for device in (sibling, over):
        pl.semaphore_signal(barrier, inc=1, device_id=device, device_id_type=MESH)
    pl.semaphore_wait(barrier, 2)

    pieces = [pl.ds(k * chunk, chunk) for k in range(CHUNKS)]
    row_copies = [
        to(over, rows_ref.at[at], rows.at[s, g, at], row_send.at[k], row_recv.at[k]) for k, at in enumerate(pieces)
    ]
    row_passes = [
        to(sibling, rows.at[s, 1 - g, at], rows.at[s, 1 - g, at], pass_send.at[k], pass_recv.at[k])
        for k, at in enumerate(pieces)
    ]
    near = [
        to(sibling, rows_ref, rows.at[s, g], near_send.at[0], near_recv.at[0]),
        to(sibling, map_ref, maps.at[s], near_send.at[1], near_recv.at[1]),
        to(sibling, piv_ref.at[s], piv_ref.at[s], near_send.at[2], near_recv.at[2]),
        to(sibling, own_ref, sib_ref, near_send.at[3], near_recv.at[3]),
    ]
    strips = [(pl.ds(r * NB, NB), pl.ds(r * NB, square - r * NB)) for r in range(done)]
    strips.append((pl.ds(square, EXTRA), pl.ds(0, square)))
    far_copies = [
        to(over, piv_ref.at[s, a, b], piv_ref.at[2, a, b], far_send.at[k], far_recv.at[k])
        for k, (a, b) in enumerate(strips)
    ]
    far_passes = [
        to(sibling, piv_ref.at[2, a, b], piv_ref.at[2, a, b], far_pass_send.at[k], far_pass_recv.at[k])
        for k, (a, b) in enumerate(strips)
    ]
    far_panel = to(over, own_ref, far_ref, panel_send, panel_recv)
    for copy in row_copies:
        copy.start()
    near[0].start()
    near[1].start()

    loads[2].wait()
    eye = lax.broadcasted_iota(jnp.int32, (NB, NB), 0) == lax.broadcasted_iota(jnp.int32, (NB, NB), 1)
    for r in range(done):
        at = slice(r * NB, (r + 1) * NB)
        for c in range(done):
            block_rc = front[pl.ds(r * NB * col_blocks + c, NB, stride=col_blocks), :]
            rounded = block_rc.astype(BF16)
            piv_ref[s, at, c * NB : (c + 1) * NB] = rounded
            if r == c:
                rest = jnp.where(eye, block_rc - rounded.astype(F32), 0.0)
                rest = jnp.broadcast_to(jnp.sum(rest, axis=0, keepdims=True), (EXTRA, NB))
                piv_ref[s, square : square + EXTRA, c * NB : (c + 1) * NB] = rest.astype(BF16)
    near[2].start()

    @pl.when(s == g)
    def _():
        for copy in far_copies:
            copy.start()

    for r in range(done):
        at = slice(r * NB, (r + 1) * NB)
        for c in range(done, col_blocks):
            block_rc = front[pl.ds(r * NB * col_blocks + c, NB, stride=col_blocks), :]
            own_ref[at, (c - done) * NB : (c - done + 1) * NB] = block_rc.astype(BF16)
    near[3].start()

    @pl.when(s == g)
    def _():
        far_panel.start()

    def spread(children, half, first, size, fresh):
        @pl.loop(0, wide_ref.shape[0] // TILE)
        def _(t):
            at = pl.ds(pl.multiple_of(t * TILE, TILE), TILE)
            for child in children:
                ids = maps[child, :, pl.ds(pl.multiple_of(half * count + first, NB), size)]
                cols = pl.ds(pl.multiple_of(child * width, NB), width)
                part = hot_dot(ids, t * TILE, rows[child, half, pl.ds(first, size), :])
                if not fresh:
                    part = part + wide_ref[at, cols].astype(F32)
                wide_ref[at, cols] = part.astype(BF16)

    loads[0].wait()
    loads[1].wait()
    spread((s,), g, 0, count, True)
    near[0].wait_recv()
    near[1].wait_recv()
    spread((1 - s,), g, 0, count, True)
    for k in range(CHUNKS):
        row_copies[k].wait_recv()
        row_passes[k].start()
        row_passes[k].wait_recv()
        spread((s, 1 - s), 1 - g, k * chunk, chunk, False)

    @pl.when(s == g)
    def _():
        for copy in far_passes:
            copy.wait_recv()
        for copy in far_copies:
            copy.wait_send()

    @pl.when(s != g)
    def _():
        for copy, passed in zip(far_copies, far_passes):
            copy.wait_recv()
            passed.start()
        for passed in far_passes:
            passed.wait_send()

    near[2].wait_recv()
    factor_pivots_paired(g, piv_ref, wide_ref, factor_ref, high_ref, low_ref, upper_ref, held, gone)

    @pl.when(s == g)
    def _():
        far_panel.wait_send()

    @pl.when(s != g)
    def _():
        far_panel.wait_recv()

    near[3].wait_recv()
    for copy in near + row_copies + row_passes:
        copy.wait_send()


def exchange_and_factor(child_map, rows, front, col_blocks):
    vmem = pl.BlockSpec(memory_space=pltpu.VMEM)
    anywhere = pl.BlockSpec(memory_space=pl.ANY)
    half = PIV // 2
    below = col_blocks * NB - half
    count, width = rows.shape
    dma = pltpu.SemaphoreType.DMA
    strips = half // NB + 1
    panel = jax.ShapeDtypeStruct((half, below), BF16)
    square = functools.partial(jax.ShapeDtypeStruct, (PIV, PIV))
    return pl.pallas_call(
        exchange_kernel,
        in_specs=[anywhere] * 3,
        out_specs=[vmem] * 8,
        out_shape=[
            jax.ShapeDtypeStruct((PF, 2 * width), BF16),
            panel, panel, panel,
            square(F32), square(BF16), square(BF16), jax.ShapeDtypeStruct((PIV, NB), F32),
        ],
        scratch_shapes=[
            pltpu.VMEM((2, 2, count, width), BF16),
            pltpu.VMEM((2, 1, child_map.shape[1]), jnp.int32),
            pltpu.VMEM((half * col_blocks, NB), F32),
            pltpu.VMEM((3, half + EXTRA, half), BF16),
            pltpu.VMEM((PIV, PIV), BF16),
            pltpu.VMEM((NB, PIV), F32),
            dma((3,)),
            dma((CHUNKS,)), dma((CHUNKS,)), dma((CHUNKS,)), dma((CHUNKS,)),
            dma((4,)), dma((4,)),
            dma((strips,)), dma((strips,)), dma((strips,)), dma((strips,)),
            dma, dma,
        ],
        compiler_params=pltpu.CompilerParams(
            collective_id=0, has_side_effects=True, vmem_limit_bytes=34 * 1024 * 1024
        ),
        name="exchange_and_factor",
    )(child_map, rows, front)


def paired_schur_kernel(
    me_ref, front_ref, own_ref, sib_ref, far_ref, rows_ref, factor_ref, high_ref, low_ref, upper_ref,
    out_ref, mycols, across, xr, other, xl,
):
    s, g = me_ref[0], me_ref[1]
    step = pl.program_id(0)
    below = own_ref.shape[1]
    half = PIV // 2
    done = half // NB
    col_blocks = done + below // NB
    per = out_ref.shape[0] // (NB * col_blocks)
    tall = per * NB
    pivot_steps = done // per

    @pl.when(step == 0)
    def _():
        for c in range(below // NB):
            mycols[c * NB : (c + 1) * NB, :] = rows_ref[block((c + done) * 2 + g), :]
        for i in range(done):
            at = slice(i * NB, (i + 1) * NB)
            both = slice(2 * i * NB, 2 * (i + 1) * NB)
            here, there = own_ref[at, :].astype(F32), sib_ref[at, :].astype(F32)
            piece = jnp.concatenate([jnp.where(s == 0, here, there), jnp.where(s == 0, there, here)], 0)
            across[both, :] = (piece - dot(rows_ref[both, :], mycols[...], NT)).astype(BF16)
            other[:, at] = jnp.where(s == g, there, far_ref[at, :].astype(F32)).T.astype(BF16)

    @pl.when(step == 1)
    def _():
        for i in range(done):
            both = slice(2 * i * NB, 2 * (i + 1) * NB)
            deep = 2 * (i + 1) * NB
            xr[both, :] = dot(high_ref[both, :deep], across[:deep, :]).astype(BF16)

    @pl.when(step < pivot_steps)
    def _():
        for p in range(per):
            row_id = 2 * (step * per + p) + s
            for c in range(col_blocks):
                to = pl.ds(p * NB * col_blocks + c, NB, stride=col_blocks)
                if c < done:
                    col_id = 2 * c + g
                    here = factor_ref[block(col_id), block(row_id)]
                    here = jnp.where(row_id == col_id, upper_ref[block(row_id), :], here)
                    out_ref[to, :] = jnp.where(row_id >= col_id, here.T, 0.0)
                else:
                    out_ref[to, :] = jnp.zeros((NB, NB), F32)

    @pl.when(step >= pivot_steps)
    def _():
        mine = jnp.concatenate([rows_ref[block(2 * (step * per + p) + s), :] for p in range(per)], 0)
        local = pl.ds(pl.multiple_of((step - pivot_steps) * tall, tall), tall)
        for c in range(done):
            for p in range(per):
                piece = front_ref[pl.ds(p * NB * col_blocks + c, NB, stride=col_blocks), :]
                xl[p * NB : (p + 1) * NB, block(2 * c + g)] = piece
            xl[:, block(2 * c + 1 - g)] = other[local, c * NB : (c + 1) * NB].astype(F32)
        a_high, a_low = split(xl[...] - dot(mine, rows_ref[:PIV, :], NT))
        for i in range(done):
            both = slice(2 * i * NB, 2 * (i + 1) * NB)
            deep = 2 * (i + 1) * NB
            l_high, l_low = high_ref[both, :deep], low_ref[both, :deep]
            xl[:, both] = dot(a_high[:, :deep], l_high, NT) + (
                dot(a_low[:, :deep], l_high, NT) + dot(a_high[:, :deep], l_low, NT)
            )
        taken = dot(mine, mycols[...], NT) + dot(xl[...].astype(BF16), xr[...])
        for p in range(per):
            at = slice(p * NB, (p + 1) * NB)
            for c in range(col_blocks):
                to = pl.ds(p * NB * col_blocks + c, NB, stride=col_blocks)
                if c < done:
                    out_ref[to, :] = xl[at, block(2 * c + g)]
                else:
                    out_ref[to, :] = front_ref[to, :] - taken[at, (c - done) * NB : (c - done + 1) * NB]


def paired_schur(me, front, own, sib, far, expanded, factor, high, low, upper, col_blocks):
    vmem = pl.BlockSpec(memory_space=pltpu.VMEM)
    per = 2
    tall = per * NB * col_blocks
    first = PIV // 2 // NB // per
    below = own.shape[1]
    tall_below = front.shape[0] // col_blocks - PIV // 2
    return pl.pallas_call(
        paired_schur_kernel,
        grid=(front.shape[0] // tall,),
        in_specs=[
            pl.BlockSpec(memory_space=pltpu.SMEM),
            pl.BlockSpec((tall, NB), lambda i: (jnp.maximum(i, first), 0)),
        ]
        + [vmem] * 8,
        out_specs=pl.BlockSpec((tall, NB), lambda i: (i, 0)),
        out_shape=jax.ShapeDtypeStruct(front.shape, F32),
        scratch_shapes=[
            pltpu.VMEM((below, expanded.shape[1]), BF16),
            pltpu.VMEM((PIV, below), BF16),
            pltpu.VMEM((PIV, below), BF16),
            pltpu.VMEM((tall_below, PIV // 2), BF16),
            pltpu.VMEM((per * NB, PIV), F32),
        ],
        compiler_params=pltpu.CompilerParams(vmem_limit_bytes=36 * 1024 * 1024),
        name="schur",
    )(me, front, own, sib, far, expanded, factor, high, low, upper)


def paired_device(front_entries, coupling_rows, child_map):
    s = lax.axis_index("sub") % 2
    g = lax.axis_index("grid")
    row_blocks, _, _, col_width = front_entries.shape[1:]
    col_blocks = col_width // NB
    front = front_entries.reshape(row_blocks * NB * col_blocks, NB)
    me = jnp.stack([s, g]).astype(jnp.int32)
    expanded, own, sib, far, factor, high, low, upper = exchange_and_factor(
        child_map, coupling_rows[0], front, col_blocks
    )
    result = paired_schur(me, front, own, sib, far, expanded, factor, high, low, upper, col_blocks)
    return result.reshape(front_entries.shape)


def solution(mesh):
    return jax.shard_map(
        paired_device if mesh.shape["grid"] == 2 else on_device,
        mesh=mesh,
        in_specs=(P("sub", None, None, "grid", None), P("sub", "grid", None), P("sub", None)),
        out_specs=P("sub", None, None, "grid", None),
        check_vma=False,
    )
```

```python
import functools

import jax
import jax.numpy as jnp
from jax import lax
from jax.experimental import pallas as pl
from jax.experimental.pallas import tpu as pltpu
from jax.sharding import PartitionSpec as P

NB = 128
PF = 3072
PIV = 1024
NPB = PIV // NB
SUBL = 8
EXTRA = 16
NT = (((1,), (1,)), ((), ()))
NN = (((1,), (0,)), ((), ()))
F32 = jnp.float32
BF16 = jnp.bfloat16


def dot(a, b, dims=NN):
    return lax.dot_general(a, b, dims, preferred_element_type=F32)


def split(x):
    high = x.astype(BF16)
    return high, (x - high.astype(F32)).astype(BF16)


def dot3(a, b, dims=NN):
    ah, al = split(a)
    bh, bl = split(b)
    return dot(ah, bh, dims) + (dot(al, bh, dims) + dot(ah, bl, dims))


def sibling_swap(shard):
    return lax.ppermute(shard, "sub", [(i, i ^ 1) for i in range(lax.axis_size("sub"))])


def ring_gather(shard):
    count = lax.axis_size("grid")
    parts = [shard]
    for k in range(1, count):
        parts.append(lax.ppermute(shard, "grid", [((i + k) % count, i) for i in range(count)]))
    return jnp.stack(parts)


def block(index):
    return pl.ds(pl.multiple_of(index * NB, NB), NB)


def expand_kernel(map_ref, rows_ref, out_ref):
    rows = out_ref.shape[0]
    width = rows_ref.shape[2]
    first = pl.program_id(0) * rows
    for child in range(2):
        ids = first + lax.broadcasted_iota(jnp.int32, (rows, map_ref.shape[2]), 0)
        hot = jnp.where(map_ref[child] == ids, 1.0, 0.0).astype(BF16)
        out_ref[:, child * width : (child + 1) * width] = dot(hot, rows_ref[child]).astype(BF16)


def expand(maps, rows):
    tile = 256
    width = rows.shape[2]
    return pl.pallas_call(
        expand_kernel,
        grid=(PF // tile,),
        in_specs=[
            pl.BlockSpec(maps.shape, lambda i: (0, 0, 0)),
            pl.BlockSpec(rows.shape, lambda i: (0, 0, 0)),
        ],
        out_specs=pl.BlockSpec((tile, 2 * width), lambda i: (i, 0)),
        out_shape=jax.ShapeDtypeStruct((PF, 2 * width), BF16),
        name="expand",
    )(maps, rows)


def factor_block(diag):
    groups = NB // SUBL
    a = [diag[v * SUBL : (v + 1) * SUBL] for v in range(groups)]
    lane = lax.broadcasted_iota(jnp.int32, (SUBL, NB), 1)
    sub = lax.broadcasted_iota(jnp.int32, (SUBL, NB), 0)

    def along(x, row):
        return jnp.broadcast_to(x[row : row + 1], (SUBL, NB))

    for t in range(groups):
        cols = [
            [jnp.broadcast_to(a[v][:, t * SUBL + l : t * SUBL + l + 1], (SUBL, NB)) for l in range(SUBL)]
            for v in range(t, groups)
        ]
        for l in range(SUBL):
            inv_pivot = 1.0 / along(cols[0][l], l)
            row = along(a[t], l) * jnp.where(lane == t * SUBL + l, 2.0, 1.0)
            ahead = [along(cols[0][k], l) for k in range(l + 1, SUBL)]
            for v in range(t, groups):
                mine = cols[v - t]
                m = mine[l] * inv_pivot
                if v == t:
                    m = jnp.where(sub > l, m, 0.0)
                a[v] = a[v] - m * row
                for k in range(l + 1, SUBL):
                    mine[k] = mine[k] - m * ahead[k - l - 1]
    d_lane = jnp.zeros((SUBL, NB), F32)
    on_diag = []
    for v in range(groups):
        on_diag.append(jnp.where(lane == v * SUBL + sub, a[v], 0.0))
        d_lane = d_lane + on_diag[v]
    inv_lane = 1.0 / jnp.sum(d_lane, axis=0, keepdims=True)
    inverse, upper = [], []
    for v in range(groups):
        scale = 1.0 / jnp.sqrt(jnp.sum(on_diag[v], axis=1, keepdims=True))
        at = v * SUBL + sub
        inverse.append(jnp.where(lane <= at, a[v] * inv_lane * scale, 0.0))
        upper.append(jnp.where(lane >= at, a[v] * scale, 0.0))
    return jnp.concatenate(inverse, 0), jnp.concatenate(upper, 0)


def pivot_kernel(grid_count, me_ref, front_ref, rows_ref, factor_ref, high_ref, low_ref, w):
    s, g = me_ref[0], me_ref[1]
    held = front_ref.shape[2] - EXTRA
    eye = lax.broadcasted_iota(jnp.int32, (NB, NB), 0) == lax.broadcasted_iota(jnp.int32, (NB, NB), 1)
    for i in range(NPB):
        at = slice(i * NB, (i + 1) * NB)
        w[at, :] = -dot(rows_ref[at, :], rows_ref[...], NT)
        from_row = lax.rem(i + s, 2)
        for b in range(NPB):
            k = lax.rem(b - g + PIV // NB * grid_count, grid_count)
            cols = slice(b // grid_count * NB, (b // grid_count + 1) * NB)
            there = slice(b * NB, (b + 1) * NB)
            piece = front_ref[from_row, k, i // 2 * NB : (i // 2 + 1) * NB, cols].astype(F32)
            if b == i:
                rest = front_ref[from_row, k, held : held + EXTRA, cols].astype(F32)[:1]
                piece = piece + jnp.where(eye, rest, 0.0)
            w[at, there] += piece

    @pl.loop(0, NPB)
    def _(j):
        at = block(j)
        inverse, upper = factor_block(w[at, at])
        factor_ref[at, at] = upper.T
        w[at, at] = jnp.where(eye, 1.0, 0.0)
        panel = dot3(inverse, w[at, :])
        w[at, :] = panel
        panel16 = panel.astype(BF16)

        @pl.loop(j + 1, NPB)
        def _(i):
            mine = block(i)
            left = w[at, mine].T
            factor_ref[mine, at] = left
            w[mine, at] = jnp.zeros((NB, NB), F32)
            w[mine, :] -= dot(left.astype(BF16), panel16)

    for i in range(NPB):
        at = slice(i * NB, (i + 1) * NB)
        keep = lax.broadcasted_iota(jnp.int32, (NB, PIV), 1) < (i + 1) * NB
        high, low = split(jnp.where(keep, w[at, :], 0.0))
        high_ref[at, :] = high
        low_ref[at, :] = low


def factor_pivots(me, fronts, expanded, grid_count):
    vmem = pl.BlockSpec(memory_space=pltpu.VMEM)
    square = functools.partial(jax.ShapeDtypeStruct, (PIV, PIV))
    return pl.pallas_call(
        functools.partial(pivot_kernel, grid_count),
        grid=(1,),
        in_specs=[
            pl.BlockSpec(memory_space=pltpu.SMEM),
            vmem,
            pl.BlockSpec((PIV, expanded.shape[1]), lambda i: (0, 0)),
        ],
        out_specs=[vmem, vmem, vmem],
        out_shape=[square(F32), square(BF16), square(BF16)],
        scratch_shapes=[pltpu.VMEM((PIV, PIV), F32)],
        cost_estimate=pl.CostEstimate(flops=40 * PIV**3, bytes_accessed=16 * PIV**2, transcendentals=0),
        name="pivots",
    )(me, fronts, expanded)


def schur_kernel(
    grid_count, me_ref, front_ref, left_ref, right_ref, rows_ref, factor_ref, high_ref, low_ref,
    out_ref, mycols, across, xr, xl,
):
    s, g = me_ref[0], me_ref[1]
    r = pl.program_id(0)
    col_blocks = out_ref.shape[0] // NB
    done = NPB // grid_count

    @pl.when(r == 0)
    def _():
        for c in range(col_blocks):
            mycols[c * NB : (c + 1) * NB, :] = rows_ref[block(c * grid_count + g), :]
        for i in range(NPB):
            at = slice(i * NB, (i + 1) * NB)
            piece = right_ref[lax.rem(i + s, 2), i // 2 * NB : (i // 2 + 1) * NB, :].astype(F32)
            across[at, :] = (piece - dot(rows_ref[at, :], mycols[done * NB :, :], NT)).astype(BF16)
        for i in range(NPB):
            at = slice(i * NB, (i + 1) * NB)
            deep = (i + 1) * NB
            xr[at, :] = dot(high_ref[at, :deep], across[:deep, :]).astype(BF16)

    row_id = 2 * r + s

    @pl.when(r < NPB // 2)
    def _():
        for c in range(col_blocks):
            to = pl.ds(c, NB, stride=col_blocks)
            if c < done:
                col_id = c * grid_count + g
                here = factor_ref[block(row_id), block(col_id)]
                out_ref[to, :] = jnp.where(row_id >= col_id, here, 0.0)
            else:
                out_ref[to, :] = jnp.zeros((NB, NB), F32)

    @pl.when(r >= NPB // 2)
    def _():
        mine = rows_ref[block(row_id), :]
        local = block(r - NPB // 2)
        for b in range(NPB):
            k = lax.rem(b - g + NPB * grid_count, grid_count)
            cols = slice(b // grid_count * NB, (b // grid_count + 1) * NB)
            xl[:, b * NB : (b + 1) * NB] = left_ref[k, local, cols].astype(F32)
        a_high, a_low = split(xl[...] - dot(mine, rows_ref[:PIV, :], NT))
        x = dot(a_high, high_ref[...], NT) + (dot(a_low, high_ref[...], NT) + dot(a_high, low_ref[...], NT))
        xl[...] = x
        x16 = x.astype(BF16)
        taken = dot(mine, mycols[done * NB :, :], NT) + dot(x16, xr[...])
        for c in range(col_blocks):
            to = pl.ds(c, NB, stride=col_blocks)
            if c < done:
                out_ref[to, :] = xl[:, block(c * grid_count + g)]
            else:
                out_ref[to, :] = front_ref[to, :] - taken[:, (c - done) * NB : (c - done + 1) * NB]


def schur(me, front, left, right, expanded, factor, high, low, grid_count, col_blocks):
    vmem = pl.BlockSpec(memory_space=pltpu.VMEM)
    tall = NB * col_blocks
    below = (col_blocks - NPB // grid_count) * NB
    return pl.pallas_call(
        functools.partial(schur_kernel, grid_count),
        grid=(front.shape[0] // tall,),
        in_specs=[
            pl.BlockSpec(memory_space=pltpu.SMEM),
            pl.BlockSpec((tall, NB), lambda i: (jnp.maximum(i, NPB // 2), 0)),
        ]
        + [vmem] * 6,
        out_specs=pl.BlockSpec((tall, NB), lambda i: (i, 0)),
        out_shape=jax.ShapeDtypeStruct(front.shape, F32),
        scratch_shapes=[
            pltpu.VMEM((col_blocks * NB, expanded.shape[1]), BF16),
            pltpu.VMEM((PIV, below), BF16),
            pltpu.VMEM((PIV, below), BF16),
            pltpu.VMEM((NB, PIV), F32),
        ],
        compiler_params=pltpu.CompilerParams(vmem_limit_bytes=56 * 1024 * 1024),
        name="schur",
    )(me, front, left, right, expanded, factor, high, low)


def on_device(front_entries, coupling_rows, child_map):
    s = lax.axis_index("sub") % 2
    g = lax.axis_index("grid")
    grid_count = lax.axis_size("grid")
    row_blocks = front_entries.shape[1]
    col_width = front_entries.shape[4]
    col_blocks = col_width // NB
    wide = front_entries.reshape(row_blocks * NB, col_width)
    front = front_entries.reshape(row_blocks * NB * col_blocks, NB)
    me = jnp.stack([s, g]).astype(jnp.int32)
    top, pivot_cols = PIV // 2, PIV // grid_count

    own_rows = ring_gather(coupling_rows[0]).reshape(-1, coupling_rows.shape[2])
    own_map = jnp.roll(child_map[0].reshape(grid_count, -1), -g, axis=0).reshape(1, -1)
    rows = jnp.stack([own_rows, sibling_swap(own_rows)])
    maps = jnp.stack([own_map, sibling_swap(own_map)])

    corner = wide[:top, :pivot_cols]
    rounded = lax.reduce_precision(corner, 8, 7)
    row_ids = (jnp.arange(top, dtype=jnp.int32) // NB * 2 + s) * NB + jnp.arange(top, dtype=jnp.int32) % NB
    spots = jnp.arange(pivot_cols, dtype=jnp.int32)
    col_ids = (spots // NB * grid_count + g) * NB + spots % NB
    rest = jnp.sum(jnp.where(row_ids[:, None] == col_ids[None, :], corner - rounded, 0.0), axis=0)
    piece = jnp.concatenate(
        [corner.astype(BF16), jnp.broadcast_to(rest.astype(BF16)[None], (EXTRA, pivot_cols))]
    )
    held = ring_gather(piece)
    pivots = jnp.stack([held, sibling_swap(held)])
    left = ring_gather(wide[top:, :pivot_cols].astype(BF16))
    over = wide[:top, pivot_cols:].astype(BF16)
    right = jnp.stack([over, sibling_swap(over)])

    expanded = expand(maps, rows)
    factor, high, low = factor_pivots(me, pivots, expanded, grid_count)
    result = schur(me, front, left, right, expanded, factor, high, low, grid_count, col_blocks)
    return result.reshape(front_entries.shape)


MESH = pl.DeviceIdType.MESH
CHUNKS = 4
TILE = 1024


SUPER = 32
TN = (((0,), (0,)), ((), ()))


def factor_pieces(diag, chores=()):
    groups = NB // SUBL
    per = SUPER // SUBL
    a = [diag[v * SUBL : (v + 1) * SUBL] for v in range(groups)]
    lane = lax.broadcasted_iota(jnp.int32, (SUBL, NB), 1)
    sub = lax.broadcasted_iota(jnp.int32, (SUBL, NB), 0)

    def along(x, row):
        return jnp.broadcast_to(x[row : row + 1], (SUBL, NB))

    zero = lax.shift_right_logical(lane, 8).astype(F32)

    def columns(rows, t):
        out = [[None] * SUBL for _ in rows]
        for l in range(SUBL):
            for n, v in enumerate(rows):
                at = t * SUBL + l
                out[n][l] = jnp.broadcast_to(a[v][:, at : at + 1], (SUBL, NB)) + zero
        return out

    inverses = []
    for start in range(0, groups, per):
        stop = start + per
        fresh = columns(range(start, stop), start)
        for t in range(start, stop):
            mine = fresh
            ready = columns((t + 1,), t + 1)[0] if t + 1 < stop else []
            by_row = jnp.zeros((SUBL, NB), F32)
            for l in range(SUBL):
                inv_pivot = 1.0 / along(mine[0][l], l)
                by_row = jnp.where(sub == l, inv_pivot, by_row)
                row = along(a[t], l) * jnp.where(lane == t * SUBL + l, 2.0, 1.0)
                ahead = [along(mine[0][k], l) for k in range(l + 1, SUBL)]
                for v in range(t, stop):
                    at = mine[v - t]
                    m = at[l] * inv_pivot
                    for k in range(l + 1, SUBL):
                        at[k] = at[k] - m * ahead[k - l - 1]
                    if v == t + 1:
                        for k in range(SUBL):
                            ready[k] = ready[k] - m * along(at[l], k)
                    if v == t:
                        m = jnp.where(sub > l, m, 0.0)
                    a[v] = a[v] - m * row
            fresh = [ready] + columns(range(t + 2, stop), t + 1) if t + 1 < stop else []
            inverses.append(by_row)
            for n in range(len(chores) * t // (groups - 2), len(chores) * (t + 1) // (groups - 2)):
                if n < len(chores):
                    chores[n]()
        if stop < groups:
            left = jnp.concatenate([a[v] * inverses[v] for v in range(start, stop)], 0)
            inside = (lane >= start * SUBL) & (lane < stop * SUBL)
            right = jnp.concatenate(
                [jnp.where(inside & (lane > v * SUBL + sub), 0.0, a[v]) for v in range(start, stop)], 0
            )
            change = dot(left.astype(BF16), right.astype(BF16), TN)
            for v in range(stop, groups):
                a[v] = jnp.where(inside, 0.0, a[v]) - change[v * SUBL : (v + 1) * SUBL]
    d_lane = jnp.zeros((SUBL, NB), F32)
    for v in range(groups):
        d_lane = d_lane + jnp.where(lane == v * SUBL + sub, inverses[v], 0.0)
    inv_lane = jnp.sum(d_lane, axis=0, keepdims=True)
    inverse, upper = [], []
    for v in range(groups):
        scale = jnp.sqrt(inverses[v])
        at = v * SUBL + sub
        inverse.append(jnp.where(lane <= at, a[v] * inv_lane * scale, 0.0))
        upper.append(jnp.where(lane >= at, a[v] * scale, 0.0))
    return jnp.concatenate(inverse, 0), jnp.concatenate(upper, 0)


def corner_rows(g, front_ref, rows_ref, factor_ref):
    rest_at = front_ref.shape[1] - EXTRA
    eye = lax.broadcasted_iota(jnp.int32, (NB, NB), 0) == lax.broadcasted_iota(jnp.int32, (NB, NB), 1)
    for i in range(NPB):
        at = slice(i * NB, (i + 1) * NB)
        if i:
            factor_ref[at, : i * NB] = jnp.zeros((NB, i * NB), F32)
        update = dot(rows_ref[at, :], rows_ref[i * NB : PIV, :], NT)
        for b in range(i, NPB):
            up = slice(i // 2 * NB, i // 2 * NB + NB), slice(b // 2 * NB, b // 2 * NB + NB)
            down = up[1], up[0]
            if i % 2 == b % 2:
                k = 2 - (2 - i % 2) * (1 - g - i % 2 + 2 * g * (i % 2))
                piece = front_ref[k, up[0], up[1]].astype(F32)
                if b == i:
                    rest = front_ref[k, rest_at : rest_at + EXTRA, up[1]].astype(F32)[:1]
                    piece = piece + jnp.where(eye, rest, 0.0)
            else:
                direct = front_ref[i % 2, up[0], up[1]].astype(F32)
                mirrored = front_ref[b % 2, down[0], down[1]].astype(F32).T
                piece = jnp.where(g == b % 2, direct, mirrored)
            factor_ref[at, b * NB : (b + 1) * NB] = piece - update[:, (b - i) * NB : (b - i + 1) * NB]


def pair(q):
    return pl.ds(pl.multiple_of(q * 2 * NB, 2 * NB), 2 * NB)


def eliminate(
    s, g, rest_ready, other_ready, piv_ref, wide_ref, front, own_ref, sib_ref, other_ref, factor_ref, upper_ref,
    left_ref, right_ref, held, gone, diag, inverse_ref, high_ref, low_ref, cols_ref, across, a_high, a_low,
):
    half = PIV // 2
    done = half // NB
    below = own_ref.shape[1]
    col_blocks = done + below // NB
    row_blocks = a_high.shape[0] // NB
    eye = lax.broadcasted_iota(jnp.int32, (NB, NB), 0) == lax.broadcasted_iota(jnp.int32, (NB, NB), 1)
    identity = jnp.where(eye, 1.0, 0.0)

    def finish(j):
        at = block(j)
        panel = dot3(inverse_ref[...], factor_ref[at, :])
        factor_ref[at, :] = panel
        held[at, :] = panel.astype(BF16)
        lane = lax.broadcasted_iota(jnp.int32, (NB, PIV), 1)
        high, low = split(jnp.where(lane < (j + 1) * NB, panel, 0.0))
        high_ref[at, :] = high
        low_ref[at, :] = low

    def update_row(j):
        at, before = block(j), block(j - 1)
        factor_ref[at, :] = factor_ref[at, :] - gone[...] - dot(held[before, at], held[before, :], TN)
        factor_ref[at, at] = identity
        held[:, at] = jnp.zeros((PIV, NB), BF16)

    def gather_row(j, n):
        cols = slice(2 * n * NB, 2 * (n + 1) * NB)
        gone[:, cols] = dot(held[:, block(lax.rem(j + 1, NPB))], held[:, cols], TN)

    def step(j, chores, first=False):
        at, after = block(j), block(lax.rem(j + 1, NPB))
        if not first:
            ahead = [lambda: finish(j - 1), lambda: update_row(j)]
            ahead += [functools.partial(gather_row, j, n) for n in range(NPB // 2)]
            chores = ahead + chores
        inverse, upper = factor_pieces(diag[...], chores)
        upper_ref[at, :] = upper
        inverse_ref[...] = inverse
        next_panel = dot3(inverse, factor_ref[at, after]).astype(BF16)
        diag[...] = factor_ref[after, after] - gone[:, after] - dot(next_panel, next_panel, TN)

    def right_panel(q, n):
        cols = slice(2 * n * NB, 2 * (n + 1) * NB)
        right_ref[pair(q), cols] = dot(high_ref[pair(q), :], across[:, cols]).astype(BF16)

    def left_panel(q, n):
        rows = slice(2 * n * NB, 2 * (n + 1) * NB)
        l_high = high_ref[pair(q), :]
        left_ref[rows, pair(q)] = dot(a_high[rows, :], l_high, NT) + (
            dot(a_low[rows, :], l_high, NT) + dot(a_high[rows, :], low_ref[pair(q), :], NT)
        )

    def panels(q):
        return [
            functools.partial(left_panel, q, n) for n in range(row_blocks // 2)
        ], [functools.partial(right_panel, q, n) for n in range(below // NB // 2)]

    def prepare_right(i):
        at = slice(i * NB, (i + 1) * NB)
        both = slice(2 * i * NB, 2 * (i + 1) * NB)
        here, there = own_ref[at, :].astype(F32), sib_ref[at, :].astype(F32)
        piece = jnp.concatenate([jnp.where(s == 0, here, there), jnp.where(s == 0, there, here)], 0)
        across[both, :] = (piece - dot(wide_ref[both, :], cols_ref[...], NT)).astype(BF16)

    def prepare_left(t):
        rows = slice(2 * t * NB, 2 * (t + 1) * NB)
        mine = jnp.concatenate([wide_ref[block(2 * (done + 2 * t + p) + s), :] for p in range(2)], 0)
        left_ref[rows, :] = dot(mine, wide_ref[:PIV, :], NT)
        for c in range(done):
            for p in range(2):
                at = slice((2 * t + p) * NB, (2 * t + p + 1) * NB)
                first = (done + 2 * t + p) * NB * col_blocks + c
                cols = block(2 * c + g)
                high, low = split(front[pl.ds(first, NB, stride=col_blocks), :] - left_ref[at, cols])
                a_high[at, cols] = high
                a_low[at, cols] = low

    corner_rows(g, piv_ref, wide_ref, factor_ref)
    diag[...] = factor_ref[:NB, :NB]
    factor_ref[:NB, :NB] = identity
    gone[...] = jnp.zeros((NB, PIV), F32)
    for c in range(below // NB):
        cols_ref[c * NB : (c + 1) * NB, :] = wide_ref[block((c + done) * 2 + g), :]
    rest_ready()
    step(0, [functools.partial(prepare_right, i) for i in range(done)], first=True)
    step(1, [functools.partial(prepare_left, t) for t in range(row_blocks // 2)])

    other_ready()
    for t in range(row_blocks // 2):
        rows = slice(2 * t * NB, 2 * (t + 1) * NB)
        for c in range(done):
            cols = block(2 * c + 1 - g)
            mirrored = other_ref[c * NB : (c + 1) * NB, rows].astype(F32).T
            high, low = split(mirrored - left_ref[rows, cols])
            a_high[rows, cols] = high
            a_low[rows, cols] = low

    @pl.loop(1, NPB // 2)
    def _(q):
        lefts, rights = panels(q - 1)
        for k in range(2):
            step(2 * q + k, lefts[k::2] + rights[k::2])

    finish(NPB - 1)
    lefts, rights = panels(NPB // 2 - 1)
    for chore in rights + lefts:
        chore()


def hot_dot(ids, first, rows):
    at = first + lax.broadcasted_iota(jnp.int32, (TILE, ids.shape[1]), 0)
    return dot(jnp.where(ids == at, 1.0, 0.0).astype(BF16), rows)


def exchange_kernel(
    map_ref, rows_ref, front_ref, wide_ref, factor_ref, upper_ref, left_ref, right_ref,
    rows, maps, front, piv_ref, own_ref, sib_ref, far_ref, held, gone, diag, inverse_ref, high_ref, low_ref,
    cols_ref, across, a_high, a_low, load, row_send, row_recv, pass_send, pass_recv, near_send, near_recv,
    far_send, far_recv, far_pass_send, far_pass_recv, panel_send, panel_recv,
):
    sub, g = lax.axis_index("sub"), lax.axis_index("grid")
    s = lax.rem(sub, 2)
    sibling, over = (sub + 1 - 2 * s, g), (sub, 1 - g)
    count, width = rows_ref.shape
    chunk = count // CHUNKS
    done = piv_ref.shape[2] // NB
    square = done * NB
    col_blocks = done + own_ref.shape[1] // NB
    top = square * col_blocks

    def to(device, src, dst, send, recv):
        return pltpu.make_async_remote_copy(
            src_ref=src, dst_ref=dst, send_sem=send, recv_sem=recv, device_id=device, device_id_type=MESH
        )

    loads = [
        pltpu.make_async_copy(rows_ref, rows.at[s, g], load.at[0]),
        pltpu.make_async_copy(map_ref, maps.at[s], load.at[1]),
        pltpu.make_async_copy(front_ref.at[pl.ds(0, top)], front.at[pl.ds(0, top)], load.at[2]),
        pltpu.make_async_copy(
            front_ref.at[pl.ds(top, front.shape[0] - top)], front.at[pl.ds(top, front.shape[0] - top)], load.at[3]
        ),
    ]
    same_panel = pltpu.make_async_copy(sib_ref, far_ref, load.at[4])
    for copy in loads:
        copy.start()
    barrier = pltpu.get_barrier_semaphore()
    for device in (sibling, over):
        pl.semaphore_signal(barrier, inc=1, device_id=device, device_id_type=MESH)
    pl.semaphore_wait(barrier, 2)

    pieces = [pl.ds(k * chunk, chunk) for k in range(CHUNKS)]
    row_copies = [
        to(over, rows_ref.at[at], rows.at[s, g, at], row_send.at[k], row_recv.at[k]) for k, at in enumerate(pieces)
    ]
    row_passes = [
        to(sibling, rows.at[s, 1 - g, at], rows.at[s, 1 - g, at], pass_send.at[k], pass_recv.at[k])
        for k, at in enumerate(pieces)
    ]
    near = [
        to(sibling, rows_ref, rows.at[s, g], near_send.at[0], near_recv.at[0]),
        to(sibling, map_ref, maps.at[s], near_send.at[1], near_recv.at[1]),
        to(sibling, piv_ref.at[s], piv_ref.at[s], near_send.at[2], near_recv.at[2]),
        to(sibling, own_ref, sib_ref, near_send.at[3], near_recv.at[3]),
    ]
    strips = [(pl.ds(r * NB, NB), pl.ds(r * NB, square - r * NB)) for r in range(done)]
    strips.append((pl.ds(square, EXTRA), pl.ds(0, square)))
    far_copies = [
        to(over, piv_ref.at[s, a, b], piv_ref.at[2, a, b], far_send.at[k], far_recv.at[k])
        for k, (a, b) in enumerate(strips)
    ]
    far_passes = [
        to(sibling, piv_ref.at[2, a, b], piv_ref.at[2, a, b], far_pass_send.at[k], far_pass_recv.at[k])
        for k, (a, b) in enumerate(strips)
    ]
    far_panel = to(over, own_ref, far_ref, panel_send, panel_recv)
    for copy in row_copies:
        copy.start()
    near[0].start()
    near[1].start()

    loads[2].wait()
    eye = lax.broadcasted_iota(jnp.int32, (NB, NB), 0) == lax.broadcasted_iota(jnp.int32, (NB, NB), 1)
    for r in range(done):
        at = slice(r * NB, (r + 1) * NB)
        for c in range(done):
            block_rc = front[pl.ds(r * NB * col_blocks + c, NB, stride=col_blocks), :]
            rounded = block_rc.astype(BF16)
            piv_ref[s, at, c * NB : (c + 1) * NB] = rounded
            if r == c:
                rest = jnp.where(eye, block_rc - rounded.astype(F32), 0.0)
                rest = jnp.broadcast_to(jnp.sum(rest, axis=0, keepdims=True), (EXTRA, NB))
                piv_ref[s, square : square + EXTRA, c * NB : (c + 1) * NB] = rest.astype(BF16)
    near[2].start()

    @pl.when(s == g)
    def _():
        for copy in far_copies:
            copy.start()

    for r in range(done):
        at = slice(r * NB, (r + 1) * NB)
        for c in range(done, col_blocks):
            block_rc = front[pl.ds(r * NB * col_blocks + c, NB, stride=col_blocks), :]
            own_ref[at, (c - done) * NB : (c - done + 1) * NB] = block_rc.astype(BF16)
    near[3].start()

    @pl.when(s == g)
    def _():
        far_panel.start()

    def spread(children, half, first, size, fresh):
        @pl.loop(0, wide_ref.shape[0] // TILE)
        def _(t):
            at = pl.ds(pl.multiple_of(t * TILE, TILE), TILE)
            for child in children:
                ids = maps[child, :, pl.ds(pl.multiple_of(half * count + first, NB), size)]
                cols = pl.ds(pl.multiple_of(child * width, NB), width)
                part = hot_dot(ids, t * TILE, rows[child, half, pl.ds(first, size), :])
                if not fresh:
                    part = part + wide_ref[at, cols].astype(F32)
                wide_ref[at, cols] = part.astype(BF16)

    loads[0].wait()
    loads[1].wait()
    spread((s,), g, 0, count, True)
    near[0].wait_recv()
    near[1].wait_recv()
    spread((1 - s,), g, 0, count, True)
    for k in range(CHUNKS):
        row_copies[k].wait_recv()
        row_passes[k].start()
        row_passes[k].wait_recv()
        spread((s, 1 - s), 1 - g, k * chunk, chunk, False)

    @pl.when(s == g)
    def _():
        for copy in far_passes:
            copy.wait_recv()
        for copy in far_copies:
            copy.wait_send()

    @pl.when(s != g)
    def _():
        for copy, passed in zip(far_copies, far_passes):
            copy.wait_recv()
            passed.start()
        for passed in far_passes:
            passed.wait_send()

    near[2].wait_recv()
    near[3].wait_recv()
    held[...] = jnp.zeros(held.shape, BF16)

    @pl.when(s == g)
    def _():
        same_panel.start()

    def other_ready():
        @pl.when(s == g)
        def _():
            same_panel.wait()
            far_panel.wait_send()

        @pl.when(s != g)
        def _():
            far_panel.wait_recv()

    eliminate(
        s, g, loads[3].wait, other_ready, piv_ref, wide_ref, front, own_ref, sib_ref, far_ref, factor_ref, upper_ref,
        left_ref, right_ref, held, gone, diag, inverse_ref, high_ref, low_ref, cols_ref, across, a_high, a_low,
    )
    for copy in near + row_copies + row_passes:
        copy.wait_send()


def exchange_and_factor(child_map, rows, front, col_blocks):
    vmem = pl.BlockSpec(memory_space=pltpu.VMEM)
    anywhere = pl.BlockSpec(memory_space=pl.ANY)
    half = PIV // 2
    below = col_blocks * NB - half
    count, width = rows.shape
    dma = pltpu.SemaphoreType.DMA
    strips = half // NB + 1
    under = front.shape[0] // col_blocks - half
    panel = pltpu.VMEM((half, below), BF16)
    squares = [pltpu.VMEM((PIV, PIV), BF16)] * 2
    return pl.pallas_call(
        exchange_kernel,
        in_specs=[anywhere] * 3,
        out_specs=[vmem] * 5,
        out_shape=[
            jax.ShapeDtypeStruct((PF, 2 * width), BF16),
            jax.ShapeDtypeStruct((PIV, PIV), F32),
            jax.ShapeDtypeStruct((PIV, NB), F32),
            jax.ShapeDtypeStruct((under, PIV), F32),
            jax.ShapeDtypeStruct((PIV, below), BF16),
        ],
        scratch_shapes=[
            pltpu.VMEM((2, 2, count, width), BF16),
            pltpu.VMEM((2, 1, child_map.shape[1]), jnp.int32),
            pltpu.VMEM(front.shape, F32),
            pltpu.VMEM((3, half + EXTRA, half), BF16),
            panel, panel, panel,
            pltpu.VMEM((PIV, PIV), BF16),
            pltpu.VMEM((NB, PIV), F32),
            pltpu.VMEM((NB, NB), F32), pltpu.VMEM((NB, NB), F32),
            *squares,
            pltpu.VMEM((below, 2 * width), BF16),
            pltpu.VMEM((PIV, below), BF16),
            pltpu.VMEM((under, PIV), BF16), pltpu.VMEM((under, PIV), BF16),
            dma((5,)),
            dma((CHUNKS,)), dma((CHUNKS,)), dma((CHUNKS,)), dma((CHUNKS,)),
            dma((4,)), dma((4,)),
            dma((strips,)), dma((strips,)), dma((strips,)), dma((strips,)),
            dma, dma,
        ],
        compiler_params=pltpu.CompilerParams(
            collective_id=0, has_side_effects=True, vmem_limit_bytes=36 * 1024 * 1024
        ),
        name="exchange_and_factor",
    )(child_map, rows, front)


def paired_schur_kernel(me_ref, front_ref, rows_ref, factor_ref, upper_ref, left_ref, right_ref, out_ref, mycols):
    s, g = me_ref[0], me_ref[1]
    step = pl.program_id(0)
    done = PIV // 2 // NB
    col_blocks = done + right_ref.shape[1] // NB
    per = out_ref.shape[0] // (NB * col_blocks)
    tall = per * NB
    pivot_steps = done // per

    @pl.when(step == 0)
    def _():
        for c in range(done, col_blocks):
            mycols[(c - done) * NB : (c - done + 1) * NB, :] = rows_ref[block(c * 2 + g), :]

    @pl.when(step < pivot_steps)
    def _():
        for p in range(per):
            row_id = 2 * (step * per + p) + s
            for c in range(col_blocks):
                to = pl.ds(p * NB * col_blocks + c, NB, stride=col_blocks)
                if c < done:
                    col_id = 2 * c + g
                    here = factor_ref[block(col_id), block(row_id)]
                    here = jnp.where(row_id == col_id, upper_ref[block(row_id), :], here)
                    out_ref[to, :] = jnp.where(row_id >= col_id, here.T, 0.0)
                else:
                    out_ref[to, :] = jnp.zeros((NB, NB), F32)

    @pl.when(step >= pivot_steps)
    def _():
        mine = jnp.concatenate([rows_ref[block(2 * (step * per + p) + s), :] for p in range(per)], 0)
        local = (step - pivot_steps) * tall
        x16 = left_ref[pl.ds(pl.multiple_of(local, tall), tall), :].astype(BF16)
        taken = dot(mine, mycols[...], NT) + dot(x16, right_ref[...])
        for p in range(per):
            at = slice(p * NB, (p + 1) * NB)
            for c in range(col_blocks):
                to = pl.ds(p * NB * col_blocks + c, NB, stride=col_blocks)
                if c < done:
                    out_ref[to, :] = left_ref[pl.ds(pl.multiple_of(local + p * NB, NB), NB), block(2 * c + g)]
                else:
                    out_ref[to, :] = front_ref[to, :] - taken[at, (c - done) * NB : (c - done + 1) * NB]


def paired_schur(me, front, expanded, factor, upper, left, right, col_blocks):
    vmem = pl.BlockSpec(memory_space=pltpu.VMEM)
    per = 2
    tall = per * NB * col_blocks
    first = PIV // 2 // NB // per
    return pl.pallas_call(
        paired_schur_kernel,
        grid=(front.shape[0] // tall,),
        in_specs=[
            pl.BlockSpec(memory_space=pltpu.SMEM),
            pl.BlockSpec((tall, NB), lambda i: (jnp.maximum(i, first), 0)),
        ]
        + [vmem] * 5,
        out_specs=pl.BlockSpec((tall, NB), lambda i: (i, 0)),
        out_shape=jax.ShapeDtypeStruct(front.shape, F32),
        scratch_shapes=[pltpu.VMEM((right.shape[1], expanded.shape[1]), BF16)],
        compiler_params=pltpu.CompilerParams(vmem_limit_bytes=36 * 1024 * 1024),
        name="schur",
    )(me, front, expanded, factor, upper, left, right)


def paired_device(front_entries, coupling_rows, child_map):
    s = lax.axis_index("sub") % 2
    g = lax.axis_index("grid")
    row_blocks, _, _, col_width = front_entries.shape[1:]
    col_blocks = col_width // NB
    front = front_entries.reshape(row_blocks * NB * col_blocks, NB)
    me = jnp.stack([s, g]).astype(jnp.int32)
    expanded, factor, upper, left, right = exchange_and_factor(child_map, coupling_rows[0], front, col_blocks)
    result = paired_schur(me, front, expanded, factor, upper, left, right, col_blocks)
    return result.reshape(front_entries.shape)


def solution(mesh):
    return jax.shard_map(
        paired_device if mesh.shape["grid"] == 2 else on_device,
        mesh=mesh,
        in_specs=(P("sub", None, None, "grid", None), P("sub", "grid", None), P("sub", None)),
        out_specs=P("sub", None, None, "grid", None),
        check_vma=False,
    )
```

```python
import functools

import jax
import jax.numpy as jnp
from jax import lax
from jax.experimental import pallas as pl
from jax.experimental.pallas import tpu as pltpu
from jax.sharding import PartitionSpec as P

NB = 128
PF = 3072
PIV = 1024
NPB = PIV // NB
SUBL = 8
EXTRA = 16
NT = (((1,), (1,)), ((), ()))
NN = (((1,), (0,)), ((), ()))
F32 = jnp.float32
BF16 = jnp.bfloat16


def dot(a, b, dims=NN):
    return lax.dot_general(a, b, dims, preferred_element_type=F32)


def split(x):
    high = x.astype(BF16)
    return high, (x - high.astype(F32)).astype(BF16)


def dot3(a, b, dims=NN):
    ah, al = split(a)
    bh, bl = split(b)
    return dot(ah, bh, dims) + (dot(al, bh, dims) + dot(ah, bl, dims))


def sibling_swap(shard):
    return lax.ppermute(shard, "sub", [(i, i ^ 1) for i in range(lax.axis_size("sub"))])


def ring_gather(shard):
    count = lax.axis_size("grid")
    parts = [shard]
    for k in range(1, count):
        parts.append(lax.ppermute(shard, "grid", [((i + k) % count, i) for i in range(count)]))
    return jnp.stack(parts)


def block(index):
    return pl.ds(pl.multiple_of(index * NB, NB), NB)


def expand_kernel(map_ref, rows_ref, out_ref):
    rows = out_ref.shape[0]
    width = rows_ref.shape[2]
    first = pl.program_id(0) * rows
    for child in range(2):
        ids = first + lax.broadcasted_iota(jnp.int32, (rows, map_ref.shape[2]), 0)
        hot = jnp.where(map_ref[child] == ids, 1.0, 0.0).astype(BF16)
        out_ref[:, child * width : (child + 1) * width] = dot(hot, rows_ref[child]).astype(BF16)


def expand(maps, rows):
    tile = 256
    width = rows.shape[2]
    return pl.pallas_call(
        expand_kernel,
        grid=(PF // tile,),
        in_specs=[
            pl.BlockSpec(maps.shape, lambda i: (0, 0, 0)),
            pl.BlockSpec(rows.shape, lambda i: (0, 0, 0)),
        ],
        out_specs=pl.BlockSpec((tile, 2 * width), lambda i: (i, 0)),
        out_shape=jax.ShapeDtypeStruct((PF, 2 * width), BF16),
        name="expand",
    )(maps, rows)


def factor_block(diag):
    groups = NB // SUBL
    a = [diag[v * SUBL : (v + 1) * SUBL] for v in range(groups)]
    lane = lax.broadcasted_iota(jnp.int32, (SUBL, NB), 1)
    sub = lax.broadcasted_iota(jnp.int32, (SUBL, NB), 0)

    def along(x, row):
        return jnp.broadcast_to(x[row : row + 1], (SUBL, NB))

    for t in range(groups):
        cols = [
            [jnp.broadcast_to(a[v][:, t * SUBL + l : t * SUBL + l + 1], (SUBL, NB)) for l in range(SUBL)]
            for v in range(t, groups)
        ]
        for l in range(SUBL):
            inv_pivot = 1.0 / along(cols[0][l], l)
            row = along(a[t], l) * jnp.where(lane == t * SUBL + l, 2.0, 1.0)
            ahead = [along(cols[0][k], l) for k in range(l + 1, SUBL)]
            for v in range(t, groups):
                mine = cols[v - t]
                m = mine[l] * inv_pivot
                if v == t:
                    m = jnp.where(sub > l, m, 0.0)
                a[v] = a[v] - m * row
                for k in range(l + 1, SUBL):
                    mine[k] = mine[k] - m * ahead[k - l - 1]
    d_lane = jnp.zeros((SUBL, NB), F32)
    on_diag = []
    for v in range(groups):
        on_diag.append(jnp.where(lane == v * SUBL + sub, a[v], 0.0))
        d_lane = d_lane + on_diag[v]
    inv_lane = 1.0 / jnp.sum(d_lane, axis=0, keepdims=True)
    inverse, upper = [], []
    for v in range(groups):
        scale = 1.0 / jnp.sqrt(jnp.sum(on_diag[v], axis=1, keepdims=True))
        at = v * SUBL + sub
        inverse.append(jnp.where(lane <= at, a[v] * inv_lane * scale, 0.0))
        upper.append(jnp.where(lane >= at, a[v] * scale, 0.0))
    return jnp.concatenate(inverse, 0), jnp.concatenate(upper, 0)


def pivot_kernel(grid_count, me_ref, front_ref, rows_ref, factor_ref, high_ref, low_ref, w):
    s, g = me_ref[0], me_ref[1]
    held = front_ref.shape[2] - EXTRA
    eye = lax.broadcasted_iota(jnp.int32, (NB, NB), 0) == lax.broadcasted_iota(jnp.int32, (NB, NB), 1)
    for i in range(NPB):
        at = slice(i * NB, (i + 1) * NB)
        w[at, :] = -dot(rows_ref[at, :], rows_ref[...], NT)
        from_row = lax.rem(i + s, 2)
        for b in range(NPB):
            k = lax.rem(b - g + PIV // NB * grid_count, grid_count)
            cols = slice(b // grid_count * NB, (b // grid_count + 1) * NB)
            there = slice(b * NB, (b + 1) * NB)
            piece = front_ref[from_row, k, i // 2 * NB : (i // 2 + 1) * NB, cols].astype(F32)
            if b == i:
                rest = front_ref[from_row, k, held : held + EXTRA, cols].astype(F32)[:1]
                piece = piece + jnp.where(eye, rest, 0.0)
            w[at, there] += piece

    @pl.loop(0, NPB)
    def _(j):
        at = block(j)
        inverse, upper = factor_block(w[at, at])
        factor_ref[at, at] = upper.T
        w[at, at] = jnp.where(eye, 1.0, 0.0)
        panel = dot3(inverse, w[at, :])
        w[at, :] = panel
        panel16 = panel.astype(BF16)

        @pl.loop(j + 1, NPB)
        def _(i):
            mine = block(i)
            left = w[at, mine].T
            factor_ref[mine, at] = left
            w[mine, at] = jnp.zeros((NB, NB), F32)
            w[mine, :] -= dot(left.astype(BF16), panel16)

    for i in range(NPB):
        at = slice(i * NB, (i + 1) * NB)
        keep = lax.broadcasted_iota(jnp.int32, (NB, PIV), 1) < (i + 1) * NB
        high, low = split(jnp.where(keep, w[at, :], 0.0))
        high_ref[at, :] = high
        low_ref[at, :] = low


def factor_pivots(me, fronts, expanded, grid_count):
    vmem = pl.BlockSpec(memory_space=pltpu.VMEM)
    square = functools.partial(jax.ShapeDtypeStruct, (PIV, PIV))
    return pl.pallas_call(
        functools.partial(pivot_kernel, grid_count),
        grid=(1,),
        in_specs=[
            pl.BlockSpec(memory_space=pltpu.SMEM),
            vmem,
            pl.BlockSpec((PIV, expanded.shape[1]), lambda i: (0, 0)),
        ],
        out_specs=[vmem, vmem, vmem],
        out_shape=[square(F32), square(BF16), square(BF16)],
        scratch_shapes=[pltpu.VMEM((PIV, PIV), F32)],
        cost_estimate=pl.CostEstimate(flops=40 * PIV**3, bytes_accessed=16 * PIV**2, transcendentals=0),
        name="pivots",
    )(me, fronts, expanded)


def schur_kernel(
    grid_count, me_ref, front_ref, left_ref, right_ref, rows_ref, factor_ref, high_ref, low_ref,
    out_ref, mycols, across, xr, xl,
):
    s, g = me_ref[0], me_ref[1]
    r = pl.program_id(0)
    col_blocks = out_ref.shape[0] // NB
    done = NPB // grid_count

    @pl.when(r == 0)
    def _():
        for c in range(col_blocks):
            mycols[c * NB : (c + 1) * NB, :] = rows_ref[block(c * grid_count + g), :]
        for i in range(NPB):
            at = slice(i * NB, (i + 1) * NB)
            piece = right_ref[lax.rem(i + s, 2), i // 2 * NB : (i // 2 + 1) * NB, :].astype(F32)
            across[at, :] = (piece - dot(rows_ref[at, :], mycols[done * NB :, :], NT)).astype(BF16)
        for i in range(NPB):
            at = slice(i * NB, (i + 1) * NB)
            deep = (i + 1) * NB
            xr[at, :] = dot(high_ref[at, :deep], across[:deep, :]).astype(BF16)

    row_id = 2 * r + s

    @pl.when(r < NPB // 2)
    def _():
        for c in range(col_blocks):
            to = pl.ds(c, NB, stride=col_blocks)
            if c < done:
                col_id = c * grid_count + g
                here = factor_ref[block(row_id), block(col_id)]
                out_ref[to, :] = jnp.where(row_id >= col_id, here, 0.0)
            else:
                out_ref[to, :] = jnp.zeros((NB, NB), F32)

    @pl.when(r >= NPB // 2)
    def _():
        mine = rows_ref[block(row_id), :]
        local = block(r - NPB // 2)
        for b in range(NPB):
            k = lax.rem(b - g + NPB * grid_count, grid_count)
            cols = slice(b // grid_count * NB, (b // grid_count + 1) * NB)
            xl[:, b * NB : (b + 1) * NB] = left_ref[k, local, cols].astype(F32)
        a_high, a_low = split(xl[...] - dot(mine, rows_ref[:PIV, :], NT))
        x = dot(a_high, high_ref[...], NT) + (dot(a_low, high_ref[...], NT) + dot(a_high, low_ref[...], NT))
        xl[...] = x
        x16 = x.astype(BF16)
        taken = dot(mine, mycols[done * NB :, :], NT) + dot(x16, xr[...])
        for c in range(col_blocks):
            to = pl.ds(c, NB, stride=col_blocks)
            if c < done:
                out_ref[to, :] = xl[:, block(c * grid_count + g)]
            else:
                out_ref[to, :] = front_ref[to, :] - taken[:, (c - done) * NB : (c - done + 1) * NB]


def schur(me, front, left, right, expanded, factor, high, low, grid_count, col_blocks):
    vmem = pl.BlockSpec(memory_space=pltpu.VMEM)
    tall = NB * col_blocks
    below = (col_blocks - NPB // grid_count) * NB
    return pl.pallas_call(
        functools.partial(schur_kernel, grid_count),
        grid=(front.shape[0] // tall,),
        in_specs=[
            pl.BlockSpec(memory_space=pltpu.SMEM),
            pl.BlockSpec((tall, NB), lambda i: (jnp.maximum(i, NPB // 2), 0)),
        ]
        + [vmem] * 6,
        out_specs=pl.BlockSpec((tall, NB), lambda i: (i, 0)),
        out_shape=jax.ShapeDtypeStruct(front.shape, F32),
        scratch_shapes=[
            pltpu.VMEM((col_blocks * NB, expanded.shape[1]), BF16),
            pltpu.VMEM((PIV, below), BF16),
            pltpu.VMEM((PIV, below), BF16),
            pltpu.VMEM((NB, PIV), F32),
        ],
        compiler_params=pltpu.CompilerParams(vmem_limit_bytes=56 * 1024 * 1024),
        name="schur",
    )(me, front, left, right, expanded, factor, high, low)


def on_device(front_entries, coupling_rows, child_map):
    s = lax.axis_index("sub") % 2
    g = lax.axis_index("grid")
    grid_count = lax.axis_size("grid")
    row_blocks = front_entries.shape[1]
    col_width = front_entries.shape[4]
    col_blocks = col_width // NB
    wide = front_entries.reshape(row_blocks * NB, col_width)
    front = front_entries.reshape(row_blocks * NB * col_blocks, NB)
    me = jnp.stack([s, g]).astype(jnp.int32)
    top, pivot_cols = PIV // 2, PIV // grid_count

    own_rows = ring_gather(coupling_rows[0]).reshape(-1, coupling_rows.shape[2])
    own_map = jnp.roll(child_map[0].reshape(grid_count, -1), -g, axis=0).reshape(1, -1)
    rows = jnp.stack([own_rows, sibling_swap(own_rows)])
    maps = jnp.stack([own_map, sibling_swap(own_map)])

    corner = wide[:top, :pivot_cols]
    rounded = lax.reduce_precision(corner, 8, 7)
    row_ids = (jnp.arange(top, dtype=jnp.int32) // NB * 2 + s) * NB + jnp.arange(top, dtype=jnp.int32) % NB
    spots = jnp.arange(pivot_cols, dtype=jnp.int32)
    col_ids = (spots // NB * grid_count + g) * NB + spots % NB
    rest = jnp.sum(jnp.where(row_ids[:, None] == col_ids[None, :], corner - rounded, 0.0), axis=0)
    piece = jnp.concatenate(
        [corner.astype(BF16), jnp.broadcast_to(rest.astype(BF16)[None], (EXTRA, pivot_cols))]
    )
    held = ring_gather(piece)
    pivots = jnp.stack([held, sibling_swap(held)])
    left = ring_gather(wide[top:, :pivot_cols].astype(BF16))
    over = wide[:top, pivot_cols:].astype(BF16)
    right = jnp.stack([over, sibling_swap(over)])

    expanded = expand(maps, rows)
    factor, high, low = factor_pivots(me, pivots, expanded, grid_count)
    result = schur(me, front, left, right, expanded, factor, high, low, grid_count, col_blocks)
    return result.reshape(front_entries.shape)


MESH = pl.DeviceIdType.MESH
CHUNKS = 2
TILE = 1024


SUPER = 32
TN = (((0,), (0,)), ((), ()))


def factor_pieces(diag, chores=()):
    groups = NB // SUBL
    per = SUPER // SUBL
    a = [diag[v * SUBL : (v + 1) * SUBL] for v in range(groups)]
    lane = lax.broadcasted_iota(jnp.int32, (SUBL, NB), 1)
    sub = lax.broadcasted_iota(jnp.int32, (SUBL, NB), 0)

    def along(x, row):
        return jnp.broadcast_to(x[row : row + 1], (SUBL, NB))

    zero = lax.shift_right_logical(lane, 8).astype(F32)

    def columns(rows, t):
        out = [[None] * SUBL for _ in rows]
        for l in range(SUBL):
            for n, v in enumerate(rows):
                at = t * SUBL + l
                out[n][l] = jnp.broadcast_to(a[v][:, at : at + 1], (SUBL, NB)) + zero
        return out

    inverses = []
    for start in range(0, groups, per):
        stop = start + per
        fresh = columns(range(start, stop), start)
        for t in range(start, stop):
            mine = fresh
            ready = columns((t + 1,), t + 1)[0] if t + 1 < stop else []
            by_row = jnp.zeros((SUBL, NB), F32)
            for l in range(SUBL):
                inv_pivot = 1.0 / along(mine[0][l], l)
                by_row = jnp.where(sub == l, inv_pivot, by_row)
                row = along(a[t], l) * jnp.where(lane == t * SUBL + l, 2.0, 1.0)
                ahead = [along(mine[0][k], l) for k in range(l + 1, SUBL)]
                for v in range(t, stop):
                    at = mine[v - t]
                    m = at[l] * inv_pivot
                    for k in range(l + 1, SUBL):
                        at[k] = at[k] - m * ahead[k - l - 1]
                    if v == t + 1:
                        for k in range(SUBL):
                            ready[k] = ready[k] - m * along(at[l], k)
                    if v == t:
                        m = jnp.where(sub > l, m, 0.0)
                    a[v] = a[v] - m * row
            fresh = [ready] + columns(range(t + 2, stop), t + 1) if t + 1 < stop else []
            inverses.append(by_row)
            for n in range(len(chores) * t // (groups - 2), len(chores) * (t + 1) // (groups - 2)):
                if n < len(chores):
                    chores[n]()
        if stop < groups:
            left = jnp.concatenate([a[v] * inverses[v] for v in range(start, stop)], 0)
            inside = (lane >= start * SUBL) & (lane < stop * SUBL)
            right = jnp.concatenate(
                [jnp.where(inside & (lane > v * SUBL + sub), 0.0, a[v]) for v in range(start, stop)], 0
            )
            change = dot(left.astype(BF16), right.astype(BF16), TN)
            for v in range(stop, groups):
                a[v] = jnp.where(inside, 0.0, a[v]) - change[v * SUBL : (v + 1) * SUBL]
    d_lane = jnp.zeros((SUBL, NB), F32)
    for v in range(groups):
        d_lane = d_lane + jnp.where(lane == v * SUBL + sub, inverses[v], 0.0)
    inv_lane = jnp.sum(d_lane, axis=0, keepdims=True)
    inverse, upper = [], []
    for v in range(groups):
        scale = jnp.sqrt(inverses[v])
        at = v * SUBL + sub
        inverse.append(jnp.where(lane <= at, a[v] * inv_lane * scale, 0.0))
        upper.append(jnp.where(lane >= at, a[v] * scale, 0.0))
    return jnp.concatenate(inverse, 0), jnp.concatenate(upper, 0)


def corner_row(i, g, front_ref, rows_ref, factor_ref):
    rest_at = front_ref.shape[1] - EXTRA
    eye = lax.broadcasted_iota(jnp.int32, (NB, NB), 0) == lax.broadcasted_iota(jnp.int32, (NB, NB), 1)
    at = slice(i * NB, (i + 1) * NB)
    if i:
        factor_ref[at, : i * NB] = jnp.zeros((NB, i * NB), F32)
    update = dot(rows_ref[at, :], rows_ref[i * NB : PIV, :], NT)
    for b in range(i, NPB):
        up = slice(i // 2 * NB, i // 2 * NB + NB), slice(b // 2 * NB, b // 2 * NB + NB)
        down = up[1], up[0]
        if i % 2 == b % 2:
            k = 2 - (2 - i % 2) * (1 - g - i % 2 + 2 * g * (i % 2))
            piece = front_ref[k, up[0], up[1]].astype(F32)
            if b == i:
                rest = front_ref[k, rest_at : rest_at + EXTRA, up[1]].astype(F32)[:1]
                piece = piece + jnp.where(eye, rest, 0.0)
        else:
            direct = front_ref[i % 2, up[0], up[1]].astype(F32)
            mirrored = front_ref[b % 2, down[0], down[1]].astype(F32).T
            piece = jnp.where(g == b % 2, direct, mirrored)
        factor_ref[at, b * NB : (b + 1) * NB] = piece - update[:, (b - i) * NB : (b - i + 1) * NB]


def pair(q):
    return pl.ds(pl.multiple_of(q * 2 * NB, 2 * NB), 2 * NB)


def eliminate(
    s, g, late, panels_ready, other_ready, piv_ref, wide_ref, front, own_ref, sib_ref, other_ref, factor_ref,
    upper_ref, left_ref, right_ref, held, gone, diag, inverse_ref, high_ref, low_ref, cols_ref, across, a_high,
):
    half = PIV // 2
    done = half // NB
    below = own_ref.shape[1]
    col_blocks = done + below // NB
    row_blocks = a_high.shape[0] // NB
    eye = lax.broadcasted_iota(jnp.int32, (NB, NB), 0) == lax.broadcasted_iota(jnp.int32, (NB, NB), 1)
    identity = jnp.where(eye, 1.0, 0.0)

    def finish(j):
        at = block(j)
        panel = dot3(inverse_ref[...], factor_ref[at, :])
        factor_ref[at, :] = panel
        held[at, :] = panel.astype(BF16)
        lane = lax.broadcasted_iota(jnp.int32, (NB, PIV), 1)
        high, low = split(jnp.where(lane < (j + 1) * NB, panel, 0.0))
        high_ref[at, :] = high
        low_ref[at, :] = low

    def update_row(j):
        at, before = block(j), block(j - 1)
        factor_ref[at, :] = factor_ref[at, :] - gone[...] - dot(held[before, at], held[before, :], TN)
        factor_ref[at, at] = identity
        held[:, at] = jnp.zeros((PIV, NB), BF16)

    def gather_row(j, n):
        cols = slice(2 * n * NB, 2 * (n + 1) * NB)
        gone[:, cols] = dot(held[:, block(lax.rem(j + 1, NPB))], held[:, cols], TN)

    def step(j, chores, first=False):
        at, after = block(j), block(lax.rem(j + 1, NPB))
        if not first:
            ahead = [lambda: finish(j - 1), lambda: update_row(j)]
            ahead += [functools.partial(gather_row, j, n) for n in range(NPB // 2)]
            chores = ahead + chores
        inverse, upper = factor_pieces(diag[...], chores)
        upper_ref[at, :] = upper
        inverse_ref[...] = inverse
        next_panel = dot3(inverse, factor_ref[at, after]).astype(BF16)
        diag[...] = factor_ref[after, after] - gone[:, after] - dot(next_panel, next_panel, TN)

    def right_panel(q, n):
        cols = slice(2 * n * NB, 2 * (n + 1) * NB)
        right_ref[pair(q), cols] = dot(high_ref[pair(q), :], across[:, cols]).astype(BF16)

    def left_panel(q, n):
        rows = slice(2 * n * NB, 2 * (n + 1) * NB)
        l_high = high_ref[pair(q), :]
        left_ref[rows, pair(q)] = dot(a_high[rows, :], l_high, NT) + dot(a_high[rows, :], low_ref[pair(q), :], NT)

    def panels(q):
        return [
            functools.partial(left_panel, q, n) for n in range(row_blocks // 2)
        ], [functools.partial(right_panel, q, n) for n in range(below // NB // 2)]

    def prepare_right(i):
        at = slice(i * NB, (i + 1) * NB)
        both = slice(2 * i * NB, 2 * (i + 1) * NB)
        here, there = own_ref[at, :].astype(F32), sib_ref[at, :].astype(F32)
        piece = jnp.concatenate([jnp.where(s == 0, here, there), jnp.where(s == 0, there, here)], 0)
        across[both, :] = (piece - dot(wide_ref[both, :], cols_ref[...], NT)).astype(BF16)

    def prepare_left(t):
        rows = slice(2 * t * NB, 2 * (t + 1) * NB)
        mine = jnp.concatenate([wide_ref[block(2 * (done + 2 * t + p) + s), :] for p in range(2)], 0)
        left_ref[rows, :] = dot(mine, wide_ref[:PIV, :], NT)
        for c in range(done):
            for p in range(2):
                at = slice((2 * t + p) * NB, (2 * t + p + 1) * NB)
                first = (done + 2 * t + p) * NB * col_blocks + c
                cols = block(2 * c + g)
                piece = front[pl.ds(first, NB, stride=col_blocks), :]
                a_high[at, cols] = (piece - left_ref[at, cols]).astype(BF16)

    def gather_columns():
        for c in range(below // NB):
            cols_ref[c * NB : (c + 1) * NB, :] = wide_ref[block((c + done) * 2 + g), :]

    corner = [functools.partial(corner_row, i, g, piv_ref, wide_ref, factor_ref) for i in range(NPB)]
    corner[0]()
    diag[...] = factor_ref[:NB, :NB]
    factor_ref[:NB, :NB] = identity
    gone[...] = jnp.zeros((NB, PIV), F32)
    lefts = [functools.partial(prepare_left, t) for t in range(row_blocks // 2)]
    step(0, corner[1:2] + late + [gather_columns] + lefts, first=True)
    panels_ready()
    step(1, corner[2:] + [functools.partial(prepare_right, i) for i in range(done)])

    @pl.loop(1, NPB // 2)
    def _(q):
        lefts, rights = panels(q - 1)
        step(2 * q, rights)

        @pl.when(q == 1)
        def _():
            other_ready()
            for t in range(row_blocks // 2):
                rows = slice(2 * t * NB, 2 * (t + 1) * NB)
                for c in range(done):
                    cols = block(2 * c + 1 - g)
                    mirrored = other_ref[c * NB : (c + 1) * NB, rows].astype(F32).T
                    a_high[rows, cols] = (mirrored - left_ref[rows, cols]).astype(BF16)

        step(2 * q + 1, lefts)

    finish(NPB - 1)
    lefts, rights = panels(NPB // 2 - 1)
    for chore in rights + lefts:
        chore()


def hot_dot(ids, first, rows):
    at = first + lax.broadcasted_iota(jnp.int32, (TILE, ids.shape[1]), 0)
    return dot(jnp.where(ids == at, 1.0, 0.0).astype(BF16), rows)


def exchange_kernel(
    map_ref, rows_ref, front_ref, wide_ref, factor_ref, upper_ref, left_ref, right_ref,
    rows, maps, front, piv_ref, own_ref, sib_ref, far_ref, held, gone, diag, inverse_ref, high_ref, low_ref,
    cols_ref, across, a_high, load, row_send, row_recv, pass_send, pass_recv, near_send, near_recv,
    far_send, far_recv, far_pass_send, far_pass_recv, panel_send, panel_recv,
):
    sub, g = lax.axis_index("sub"), lax.axis_index("grid")
    s = lax.rem(sub, 2)
    sibling, over = (sub + 1 - 2 * s, g), (sub, 1 - g)
    count, width = rows_ref.shape
    chunk = count // CHUNKS
    done = piv_ref.shape[2] // NB
    square = done * NB
    col_blocks = done + own_ref.shape[1] // NB
    top = square * col_blocks

    def to(device, src, dst, send, recv):
        return pltpu.make_async_remote_copy(
            src_ref=src, dst_ref=dst, send_sem=send, recv_sem=recv, device_id=device, device_id_type=MESH
        )

    loads = [
        pltpu.make_async_copy(rows_ref, rows.at[s, g], load.at[0]),
        pltpu.make_async_copy(map_ref, maps.at[s], load.at[1]),
        pltpu.make_async_copy(front_ref.at[pl.ds(0, top)], front.at[pl.ds(0, top)], load.at[2]),
        pltpu.make_async_copy(
            front_ref.at[pl.ds(top, front.shape[0] - top)], front.at[pl.ds(top, front.shape[0] - top)], load.at[3]
        ),
    ]
    same_panel = pltpu.make_async_copy(sib_ref, far_ref, load.at[4])
    for copy in loads:
        copy.start()
    barrier = pltpu.get_barrier_semaphore()
    for device in (sibling, over):
        pl.semaphore_signal(barrier, inc=1, device_id=device, device_id_type=MESH)
    pl.semaphore_wait(barrier, 2)

    pieces = [pl.ds(k * chunk, chunk) for k in range(CHUNKS)]
    row_copies = [
        to(over, rows_ref.at[at], rows.at[s, g, at], row_send.at[k], row_recv.at[k]) for k, at in enumerate(pieces)
    ]
    row_passes = [
        to(sibling, rows.at[s, 1 - g, at], rows.at[s, 1 - g, at], pass_send.at[k], pass_recv.at[k])
        for k, at in enumerate(pieces)
    ]
    near = [
        to(sibling, rows_ref, rows.at[s, g], near_send.at[0], near_recv.at[0]),
        to(sibling, map_ref, maps.at[s], near_send.at[1], near_recv.at[1]),
        to(sibling, piv_ref.at[s], piv_ref.at[s], near_send.at[2], near_recv.at[2]),
        to(sibling, own_ref, sib_ref, near_send.at[3], near_recv.at[3]),
    ]
    strips = [(pl.ds(r * NB, NB), pl.ds(r * NB, square - r * NB)) for r in range(done)]
    strips.append((pl.ds(square, EXTRA), pl.ds(0, square)))
    far_copies = [
        to(over, piv_ref.at[s, a, b], piv_ref.at[2, a, b], far_send.at[k], far_recv.at[k])
        for k, (a, b) in enumerate(strips)
    ]
    far_passes = [
        to(sibling, piv_ref.at[2, a, b], piv_ref.at[2, a, b], far_pass_send.at[k], far_pass_recv.at[k])
        for k, (a, b) in enumerate(strips)
    ]
    far_panel = to(over, own_ref, far_ref, panel_send, panel_recv)
    for copy in row_copies:
        copy.start()
    near[0].start()
    near[1].start()

    loads[2].wait()
    eye = lax.broadcasted_iota(jnp.int32, (NB, NB), 0) == lax.broadcasted_iota(jnp.int32, (NB, NB), 1)
    for r in range(done):
        at = slice(r * NB, (r + 1) * NB)
        for c in range(done):
            block_rc = front[pl.ds(r * NB * col_blocks + c, NB, stride=col_blocks), :]
            rounded = block_rc.astype(BF16)
            piv_ref[s, at, c * NB : (c + 1) * NB] = rounded
            if r == c:
                rest = jnp.where(eye, block_rc - rounded.astype(F32), 0.0)
                rest = jnp.broadcast_to(jnp.sum(rest, axis=0, keepdims=True), (EXTRA, NB))
                piv_ref[s, square : square + EXTRA, c * NB : (c + 1) * NB] = rest.astype(BF16)
    near[2].start()

    @pl.when(s == g)
    def _():
        for copy in far_copies:
            copy.start()

    for r in range(done):
        at = slice(r * NB, (r + 1) * NB)
        for c in range(done, col_blocks):
            block_rc = front[pl.ds(r * NB * col_blocks + c, NB, stride=col_blocks), :]
            own_ref[at, (c - done) * NB : (c - done + 1) * NB] = block_rc.astype(BF16)
    @pl.when(s == g)
    def _():
        far_panel.start()

    def spread_tile(child, half, first, size, fresh, t):
        at = pl.ds(pl.multiple_of(t * TILE, TILE), TILE)
        ids = maps[child, :, pl.ds(pl.multiple_of(half * count + first, NB), size)]
        cols = pl.ds(pl.multiple_of(child * width, NB), width)
        part = hot_dot(ids, t * TILE, rows[child, half, pl.ds(first, size), :])
        if not fresh:
            part = part + wide_ref[at, cols].astype(F32)
        wide_ref[at, cols] = part.astype(BF16)

    tiles = wide_ref.shape[0] // TILE

    def spread(children, half, first, size, fresh, stop=tiles):
        @pl.loop(0, stop)
        def _(t):
            for child in children:
                spread_tile(child, half, first, size, fresh, t)

    near[3].start()
    loads[0].wait()
    loads[1].wait()
    spread((s,), g, 0, count, True)
    near[0].wait_recv()
    near[1].wait_recv()
    spread((1 - s,), g, 0, count, True)
    for k in range(CHUNKS):
        row_copies[k].wait_recv()
        row_passes[k].start()
        row_passes[k].wait_recv()
        spread((s, 1 - s), 1 - g, k * chunk, chunk, False, PIV // TILE if k == CHUNKS - 1 else tiles)
    late = [
        functools.partial(spread_tile, child, 1 - g, count - chunk, chunk, False, t)
        for t in range(PIV // TILE, tiles)
        for child in (s, 1 - s)
    ]

    @pl.when(s == g)
    def _():
        for copy in far_passes:
            copy.wait_recv()
        for copy in far_copies:
            copy.wait_send()

    @pl.when(s != g)
    def _():
        for copy, passed in zip(far_copies, far_passes):
            copy.wait_recv()
            passed.start()
        for passed in far_passes:
            passed.wait_send()

    near[2].wait_recv()
    held[...] = jnp.zeros(held.shape, BF16)
    loads[3].wait()

    def panels_ready():
        near[3].wait_recv()

        @pl.when(s == g)
        def _():
            same_panel.start()

    def other_ready():
        @pl.when(s == g)
        def _():
            same_panel.wait()
            far_panel.wait_send()

        @pl.when(s != g)
        def _():
            far_panel.wait_recv()

    eliminate(
        s, g, late, panels_ready, other_ready, piv_ref, wide_ref, front, own_ref, sib_ref, far_ref, factor_ref,
        upper_ref, left_ref, right_ref, held, gone, diag, inverse_ref, high_ref, low_ref, cols_ref, across, a_high,
    )
    for copy in near + row_copies + row_passes:
        copy.wait_send()


def exchange_and_factor(child_map, rows, front, col_blocks):
    vmem = pl.BlockSpec(memory_space=pltpu.VMEM)
    anywhere = pl.BlockSpec(memory_space=pl.ANY)
    half = PIV // 2
    below = col_blocks * NB - half
    count, width = rows.shape
    dma = pltpu.SemaphoreType.DMA
    strips = half // NB + 1
    under = front.shape[0] // col_blocks - half
    panel = pltpu.VMEM((half, below), BF16)
    squares = [pltpu.VMEM((PIV, PIV), BF16)] * 2
    return pl.pallas_call(
        exchange_kernel,
        in_specs=[anywhere] * 3,
        out_specs=[vmem] * 5,
        out_shape=[
            jax.ShapeDtypeStruct((PF, 2 * width), BF16),
            jax.ShapeDtypeStruct((PIV, PIV), F32),
            jax.ShapeDtypeStruct((PIV, NB), F32),
            jax.ShapeDtypeStruct((under, PIV), F32),
            jax.ShapeDtypeStruct((PIV, below), BF16),
        ],
        scratch_shapes=[
            pltpu.VMEM((2, 2, count, width), BF16),
            pltpu.VMEM((2, 1, child_map.shape[1]), jnp.int32),
            pltpu.VMEM(front.shape, F32),
            pltpu.VMEM((3, half + EXTRA, half), BF16),
            panel, panel, panel,
            pltpu.VMEM((PIV, PIV), BF16),
            pltpu.VMEM((NB, PIV), F32),
            pltpu.VMEM((NB, NB), F32), pltpu.VMEM((NB, NB), F32),
            *squares,
            pltpu.VMEM((below, 2 * width), BF16),
            pltpu.VMEM((PIV, below), BF16),
            pltpu.VMEM((under, PIV), BF16),
            dma((5,)),
            dma((CHUNKS,)), dma((CHUNKS,)), dma((CHUNKS,)), dma((CHUNKS,)),
            dma((4,)), dma((4,)),
            dma((strips,)), dma((strips,)), dma((strips,)), dma((strips,)),
            dma, dma,
        ],
        compiler_params=pltpu.CompilerParams(
            collective_id=0, has_side_effects=True, vmem_limit_bytes=36 * 1024 * 1024
        ),
        name="exchange_and_factor",
    )(child_map, rows, front)


def paired_schur_kernel(me_ref, front_ref, rows_ref, factor_ref, upper_ref, left_ref, right_ref, out_ref, mycols):
    s, g = me_ref[0], me_ref[1]
    step = pl.program_id(0)
    done = PIV // 2 // NB
    col_blocks = done + right_ref.shape[1] // NB
    per = out_ref.shape[0] // (NB * col_blocks)
    tall = per * NB
    pivot_steps = done // per

    @pl.when(step == 0)
    def _():
        for c in range(done, col_blocks):
            mycols[(c - done) * NB : (c - done + 1) * NB, :] = rows_ref[block(c * 2 + g), :]

    @pl.when(step < pivot_steps)
    def _():
        for p in range(per):
            row_id = 2 * (step * per + p) + s
            for c in range(col_blocks):
                to = pl.ds(p * NB * col_blocks + c, NB, stride=col_blocks)
                if c < done:
                    col_id = 2 * c + g
                    here = factor_ref[block(col_id), block(row_id)]
                    here = jnp.where(row_id == col_id, upper_ref[block(row_id), :], here)
                    out_ref[to, :] = jnp.where(row_id >= col_id, here.T, 0.0)
                else:
                    out_ref[to, :] = jnp.zeros((NB, NB), F32)

    @pl.when(step >= pivot_steps)
    def _():
        mine = jnp.concatenate([rows_ref[block(2 * (step * per + p) + s), :] for p in range(per)], 0)
        local = (step - pivot_steps) * tall
        x16 = left_ref[pl.ds(pl.multiple_of(local, tall), tall), :].astype(BF16)
        taken = dot(mine, mycols[...], NT) + dot(x16, right_ref[...])
        for p in range(per):
            at = slice(p * NB, (p + 1) * NB)
            for c in range(col_blocks):
                to = pl.ds(p * NB * col_blocks + c, NB, stride=col_blocks)
                if c < done:
                    out_ref[to, :] = left_ref[pl.ds(pl.multiple_of(local + p * NB, NB), NB), block(2 * c + g)]
                else:
                    out_ref[to, :] = front_ref[to, :] - taken[at, (c - done) * NB : (c - done + 1) * NB]


def paired_schur(me, front, expanded, factor, upper, left, right, col_blocks):
    vmem = pl.BlockSpec(memory_space=pltpu.VMEM)
    per = PIV // 2 // NB
    tall = per * NB * col_blocks
    first = PIV // 2 // NB // per
    return pl.pallas_call(
        paired_schur_kernel,
        grid=(front.shape[0] // tall,),
        in_specs=[
            pl.BlockSpec(memory_space=pltpu.SMEM),
            pl.BlockSpec((tall, NB), lambda i: (jnp.maximum(i, first), 0)),
        ]
        + [vmem] * 5,
        out_specs=pl.BlockSpec((tall, NB), lambda i: (i, 0)),
        out_shape=jax.ShapeDtypeStruct(front.shape, F32),
        scratch_shapes=[pltpu.VMEM((right.shape[1], expanded.shape[1]), BF16)],
        compiler_params=pltpu.CompilerParams(vmem_limit_bytes=36 * 1024 * 1024),
        name="schur",
    )(me, front, expanded, factor, upper, left, right)


def paired_device(front_entries, coupling_rows, child_map):
    s = lax.axis_index("sub") % 2
    g = lax.axis_index("grid")
    row_blocks, _, _, col_width = front_entries.shape[1:]
    col_blocks = col_width // NB
    front = front_entries.reshape(row_blocks * NB * col_blocks, NB)
    me = jnp.stack([s, g]).astype(jnp.int32)
    expanded, factor, upper, left, right = exchange_and_factor(child_map, coupling_rows[0], front, col_blocks)
    result = paired_schur(me, front, expanded, factor, upper, left, right, col_blocks)
    return result.reshape(front_entries.shape)


def solution(mesh):
    return jax.shard_map(
        paired_device if mesh.shape["grid"] == 2 else on_device,
        mesh=mesh,
        in_specs=(P("sub", None, None, "grid", None), P("sub", "grid", None), P("sub", None)),
        out_specs=P("sub", None, None, "grid", None),
        check_vma=False,
    )
```
